32 devices in a mesh: group: 2 (over y), ctx: 4 (over z), feat: 2 (over x), ex: 2 (over core).
Axes of the slice: x: 2, y: 2, z: 4, core: 2. Of those that a mesh axis runs over, the one named last changes fastest.
Arguments:
- hidden: bfloat16 [8, 512, 8192], P(('group', 'feat', 'ex'), 'ctx'), parts along dimension 0, may hold values from -6 to 6
- cotangent: bfloat16 [8, 512, 1024], P(('group', 'feat', 'ex'), 'ctx'), parts along dimension 0, may hold values from -6 to 6
- adapter_down_factor: bfloat16 [8192, 16], replicated, may hold values from -0.0625 to 0.0625
- projection: bfloat16 [16384, 8192], P('ctx', 'feat'), may hold values from -6 to 6
- lengths: int32 [8], P(('group', 'feat', 'ex')), parts along dimension 0, may hold values from 128 to 512, as said below
- slot_example_order: int32 [8], P('group'), parts along dimension 0, may hold values from 0 to 3, each once
Outputs:
- features: float32 [8, 8192], P(('group', 'ex'), 'feat'), parts along dimension 0
The draws below stay inside these ranges and needn't reach their ends.
There are 2 independent parts, one for each index of `group`. The reference program is written for one: setup_inputs(seed, part) draws one part's arguments, and reference() takes and returns one part's arrays. A program takes and returns all parts, laid end to end along the dimension named above; an argument that names none is the same for every part. Nothing has to cross between parts.
Inputs may be any that keep to these rules, and one draw needn't show every extreme that they name: `lengths`: some example has exactly 512 valid positions and some exactly one quarter of 512.
All inputs are finite; a program needn't handle non-finite values.
Results may differ from the reference program's by a relative error of at most 0.0042.
Values may be sent and summed in bfloat16 or wider, within the bound.
No kernel may reach another device: no remote copies, remote signals or barrier semaphores. Data moves between devices by JAX's collectives and lax.ppermute only.
A program may use at most 64 MiB of HBM per device.

```python
import jax
import jax.numpy as jnp
from jax import lax

MODEL_DIM = 8192
KVW = 1024
ADAPTER_RANK = 16
FEATS = 8192
GRAD = 16384
LEN = 512
NEX = 4


def draw_lengths(key, part):
    first_key, second_key = jax.random.split(jax.random.fold_in(key, 11))
    base = jax.random.randint(first_key, (NEX,), LEN // 4, LEN + 1)
    chosen = jax.random.permutation(second_key, NEX)
    base = base.at[chosen[0]].set(LEN)
    base = base.at[chosen[1]].set(LEN // 4)
    return base.astype(jnp.int32)


def draw_projection(key, part):
    keys = jax.random.split(jax.random.fold_in(key, 23), 2)
    ramp = jnp.arange(FEATS, dtype=jnp.float32) / FEATS
    jitter = jax.random.uniform(keys[0], (FEATS,), jnp.float32)
    column_entry = 10.0 ** (0.5 * ramp + 0.5 * jitter)
    entries = jnp.clip(jax.random.normal(keys[1], (GRAD, FEATS), jnp.float32), -4.5, 4.5)
    values = entries * column_entry[None, :] / jnp.sqrt(jnp.float32(GRAD))
    return jnp.clip(values, -6.0, 6.0).astype(jnp.bfloat16)


def block_scale(own_key, shape, shards, least, high):
    gain = 1.0
    for dim, shards_of in shards:
        heights = jax.random.uniform(jax.random.fold_in(jax.random.fold_in(own_key, 6), dim), (shards_of,), jnp.float32, least / len(shards), high / len(shards))
        gain = gain * jnp.repeat(jnp.exp(heights), shape[dim] // shards_of).reshape((-1,) + (1,) * (len(shape) - 1 - dim))
    return gain


def normal_values(stream_key, dims, deviation, bound, pieces=(), held_as=jnp.bfloat16):
    array = jax.random.normal(stream_key, dims, jnp.float32) * deviation
    if len(pieces) > 0:
        array = block_scale(stream_key, dims, pieces, -0.22, 0.18) * array
    return jnp.clip(array, min=-bound, max=bound).astype(held_as)


def setup_inputs(seed: int = 0, part: int = 0) -> dict:
    arg_keys = jax.random.split(jax.random.key(seed), 7)
    part_splits = jax.random.split(jax.random.fold_in(arg_keys[6], part), 7)
    hidden = normal_values(part_splits[0], (NEX, LEN, MODEL_DIM), 1.0, 6.0, ((0, 4), (1, 4)))
    cotangent = normal_values(part_splits[1], (NEX, LEN, KVW), 1.0, 6.0, ((0, 4), (1, 4)))
    adapter_down_factor = normal_values(arg_keys[2], (MODEL_DIM, ADAPTER_RANK), MODEL_DIM ** -0.5, 0.0625)
    projection = draw_projection(jax.random.fold_in(arg_keys[6], 71), part)
    lengths = draw_lengths(jax.random.fold_in(jax.random.fold_in(arg_keys[6], part), 71), part)
    slot_example_order = jax.random.permutation(part_splits[5], NEX).astype(jnp.int32)
    return dict(hidden=hidden, cotangent=cotangent, adapter_down_factor=adapter_down_factor, projection=projection, lengths=lengths, slot_example_order=slot_example_order)


def reference(hidden, cotangent, adapter_down_factor, projection, lengths, slot_example_order):
    flattened_rows = hidden.reshape(NEX * LEN, MODEL_DIM)
    down_factor_rows = jnp.dot(flattened_rows, adapter_down_factor, preferred_element_type=jnp.float32).astype(jnp.bfloat16)
    down_factor_rows = down_factor_rows.reshape(NEX, LEN, ADAPTER_RANK)
    position = jnp.arange(LEN, dtype=jnp.int32)
    retain_mask = (position[None, :] < lengths[:, None]).astype(jnp.bfloat16)
    down_factor_rows = down_factor_rows * retain_mask[:, :, None]
    grad = jnp.einsum('ntr,ntj->nrj', down_factor_rows.astype(jnp.float32), cotangent.astype(jnp.float32))
    grad_rows = grad.reshape(NEX, GRAD).astype(jnp.bfloat16)
    projected = jnp.dot(grad_rows, projection, preferred_element_type=jnp.float32)
    scaled = projected / jnp.sqrt(lax.optimization_barrier(jnp.mean(projected * projected, axis=1, keepdims=True)) + 1e-06)
    example_ids = jnp.arange(NEX, dtype=jnp.int32)
    select = (slot_example_order[None, :] == example_ids[:, None]).astype(jnp.float32)
    return jnp.dot(select, scaled, precision=lax.Precision.HIGHEST, preferred_element_type=jnp.float32)
```

```python
import jax
import jax.numpy as jnp
from jax import lax
from jax.experimental import pallas as pl
from jax.experimental.pallas import tpu as pltpu
from jax.sharding import PartitionSpec as P

FEATS = 8192


def partner_pairs(count, step):
    if count & (count - 1) == 0:
        return [(i, i ^ step) for i in range(count)]
    return [(i, (i + step) % count) for i in range(count)]


def target_of(index, count, step):
    if count & (count - 1) == 0:
        return index ^ step
    return lax.rem(index + step, count)


def source_of(index, count, step):
    if count & (count - 1) == 0:
        return index ^ step
    return lax.rem(index + count - step, count)


def swap(value, axis, count, step):
    return lax.ppermute(value, axis, partner_pairs(count, step))


def project_body(half_ref, rows_ref, projection_ref, out_ref):
    part = jnp.dot(rows_ref[...], projection_ref[...], preferred_element_type=jnp.float32)

    @pl.when(pl.program_id(0) == 0)
    def _():
        out_ref[...] = part

    @pl.when(pl.program_id(0) > 0)
    def _():
        out_ref[...] += part


def project(rows, projection, part_index, parts):
    depth, width = projection.shape
    own_width = width // parts
    block = min(512, depth)
    return pl.pallas_call(
        project_body,
        out_shape=jax.ShapeDtypeStruct((rows.shape[0], own_width), jnp.float32),
        grid_spec=pltpu.PrefetchScalarGridSpec(
            num_scalar_prefetch=1,
            grid=(depth // block,),
            in_specs=[
                pl.BlockSpec((rows.shape[0], block), lambda k, part: (0, k)),
                pl.BlockSpec((block, own_width), lambda k, part: (k, part[0])),
            ],
            out_specs=pl.BlockSpec((rows.shape[0], own_width), lambda k, part: (0, 0)),
        ),
    )(part_index, rows, projection)


def per_device(hidden, cotangent, adapter_down_factor, projection, lengths, slot_example_order):
    ctx_count = lax.axis_size("ctx")
    feat_count = lax.axis_size("feat")
    ex_count = lax.axis_size("ex")
    ctx, feat, ex = lax.axis_index("ctx"), lax.axis_index("feat"), lax.axis_index("ex")
    own, token_count, model_width = hidden.shape
    down_rows = jnp.dot(
        hidden.reshape(own * token_count, model_width),
        adapter_down_factor,
        preferred_element_type=jnp.float32,
    )
    down_rows = down_rows.astype(jnp.bfloat16).reshape(own, token_count, -1)
    position = ctx * token_count + lax.iota(jnp.int32, token_count)
    retain_mask = (position[None, :] < lengths[:, None]).astype(jnp.bfloat16)
    down_rows = down_rows * retain_mask[:, :, None]
    partial = jnp.einsum("etr,etj->erj", down_rows, cotangent, preferred_element_type=jnp.float32)

    blocks = partial.reshape(own, ctx_count, -1)
    block = lambda index: lax.dynamic_index_in_dim(blocks, index, 1, keepdims=False)
    grad = block(ctx)
    for step in range(1, ctx_count):
        grad = grad + swap(block(target_of(ctx, ctx_count, step)), "ctx", ctx_count, step)
    grad_rows = grad.astype(jnp.bfloat16)

    slots = slot_example_order.reshape(feat_count, ex_count, own)
    ex_parts = [grad_rows]
    ex_places = [ex]
    for step in range(1, ex_count):
        ex_parts.append(swap(grad_rows, "ex", ex_count, step))
        ex_places.append(source_of(ex, ex_count, step))
    of_chip = jnp.concatenate(ex_parts, axis=0)
    parts, ids = [of_chip], [jnp.concatenate([slots[feat, e] for e in ex_places])]
    for step in range(1, feat_count):
        parts.append(swap(of_chip, "feat", feat_count, step))
        place = source_of(feat, feat_count, step)
        ids.append(jnp.concatenate([slots[place, e] for e in ex_places]))
    everything = jnp.concatenate(parts, axis=0)
    held = jnp.concatenate(ids)
    count = everything.shape[0]
    select = (held[None, :] == lax.iota(jnp.int32, count)[:, None]).astype(jnp.bfloat16)
    ordered = jnp.dot(select, everything, preferred_element_type=jnp.float32).astype(jnp.bfloat16)

    product = project(ordered, projection, ex.astype(jnp.int32)[None], ex_count)
    per_ex = product.reshape(ex_count, count // ex_count, -1)
    row_part = lambda index: lax.dynamic_index_in_dim(per_ex, index, 0, keepdims=False)
    column_parts, column_places = [row_part(ex)], [ex]
    for step in range(1, ex_count):
        column_parts.append(swap(row_part(target_of(ex, ex_count, step)), "ex", ex_count, step))
        column_places.append(source_of(ex, ex_count, step))
    mine = jnp.stack(column_parts, axis=1)
    summed = mine
    for step in range(1, ctx_count):
        summed = summed + swap(mine, "ctx", ctx_count, step)
    own_squares = jnp.sum(summed * summed, axis=(1, 2))
    squares = own_squares
    for step in range(1, feat_count):
        squares = squares + swap(own_squares, "feat", feat_count, step)
    scaled = summed / jnp.sqrt(squares / FEATS + 1e-06)[:, None, None]
    placed = jnp.stack(column_places)
    ordered_columns = sum(
        jnp.where((placed[k] == lax.iota(jnp.int32, ex_count))[None, :, None], scaled[:, k : k + 1], 0.0)
        for k in range(ex_count)
    )
    return ordered_columns.reshape(scaled.shape[0], -1)


def solution(mesh):
    in_specs = (
        P(("group", "feat", "ex"), "ctx", None),
        P(("group", "feat", "ex"), "ctx", None),
        P(),
        P("ctx", "feat"),
        P(("group", "feat", "ex")),
        P("group"),
    )
    out_specs = P(("group", "ex"), "feat")
    return jax.shard_map(
        per_device, mesh=mesh, in_specs=in_specs, out_specs=out_specs, check_vma=False
    )
```

```python
import functools
import itertools

import jax
import jax.numpy as jnp
from jax import lax
from jax.experimental import pallas as pl
from jax.experimental.pallas import tpu as pltpu
from jax.sharding import PartitionSpec as P

MIB = 1 << 20
SHARES = (1, 3, 2, 2)
VMEM = pl.BlockSpec(memory_space=pltpu.VMEM)
HBM = pl.BlockSpec(memory_space=pltpu.HBM)


def is_power(count):
    return count & (count - 1) == 0


def place_at(index, count, step, sign=1):
    if is_power(count):
        return index ^ step
    return (index + sign * step + count) % count


def step_to(index, target, count):
    if is_power(count):
        return index ^ target
    return lax.rem(target - index + count, count)


def swap(value, axes, steps):
    sizes = [lax.axis_size(a) for a in axes]
    flat = lambda place: functools.reduce(lambda total, p: total * p[1] + p[0], zip(place, sizes), 0)
    pairs = [
        (flat(place), flat([place_at(i, n, s) for i, n, s in zip(place, sizes, steps)]))
        for place in itertools.product(*map(range, sizes))
    ]
    return lax.ppermute(value, tuple(axes) if len(axes) > 1 else axes[0], pairs)


def params(mib, **more):
    return pltpu.CompilerParams(vmem_limit_bytes=mib * MIB, **more)


def lane_dot(a, b):
    return lax.dot_general(a, b, (((1,), (1,)), ((), ())), preferred_element_type=jnp.float32)


def hbm(value):
    return pltpu.with_memory_space_constraint(value, pltpu.HBM)


def share_rows(depth, number):
    eighth = depth // sum(SHARES)
    return sum(SHARES[:number]) * eighth, SHARES[number] * eighth


def share_copy(projection_hbm, buffer, sem, number):
    first, rows = share_rows(projection_hbm.shape[0], number)
    width = buffer.shape[1]
    columns = pl.ds(pl.multiple_of(lax.axis_index("ex") * width, 128), width)
    return pltpu.make_async_copy(projection_hbm.at[pl.ds(first, rows), columns], buffer, sem)


def share_shape(projection, number, ex_count):
    depth, width = projection.shape
    return share_rows(depth, number)[1], width // ex_count


def load_body(number, after_ref, projection_hbm, buffer, sem):
    copy = share_copy(projection_hbm, buffer, sem, number)
    copy.start()
    copy.wait()


def load(projection, number, ex_count, after):
    return pl.pallas_call(
        functools.partial(load_body, number),
        out_shape=pltpu.VMEM(share_shape(projection, number, ex_count), projection.dtype),
        in_specs=[VMEM, HBM],
        out_specs=VMEM,
        scratch_shapes=[pltpu.SemaphoreType.DMA],
        compiler_params=params(2),
    )(after, hbm(projection))


def gradient_body(chunks, counts, hidden_hbm, factor_hbm, cotangent_hbm, projection_hbm, lengths, order_hbm, *refs):
    ctx_count, feat_count, ex_count = counts
    outs, ranks_ref, share_ref = refs[:ctx_count], refs[ctx_count], refs[ctx_count + 1]
    hidden, factor, cotangent, blocks, order, sems, order_sem = refs[ctx_count + 2 :]
    own, tokens, width = hidden.shape
    part = width // chunks
    order_copy = pltpu.make_async_copy(order_hbm, order, order_sem)
    order_copy.start()
    copies = [pltpu.make_async_copy(factor_hbm, factor, sems.at[0])]
    for k in range(chunks):
        columns = pl.ds(k * part, part)
        copies.append(
            pltpu.make_async_copy(hidden_hbm.at[:, :, columns], hidden.at[:, :, columns], sems.at[1 + k])
        )
    copies.append(pltpu.make_async_copy(cotangent_hbm, cotangent, sems.at[1 + chunks]))
    copies.append(share_copy(projection_hbm, share_ref, sems.at[2 + chunks], 0))
    for copy in copies:
        copy.start()
    copies[0].wait()
    down = [None] * own
    for k in range(chunks):
        copies[1 + k].wait()
        for e in range(own):
            product = lane_dot(factor[:, k * part : (k + 1) * part], hidden[e, :, k * part : (k + 1) * part])
            down[e] = product if k == 0 else down[e] + product
    copies[-2].wait()
    order_copy.wait()
    place = lax.axis_index("ctx")
    for e in range(own):
        rows = down[e].astype(jnp.bfloat16)
        position = place * tokens + lax.broadcasted_iota(jnp.int32, rows.shape, 1)
        rows = jnp.where(position < lengths[e], rows.astype(jnp.float32), 0.0).astype(jnp.bfloat16)
        grad = jnp.dot(rows, cotangent[e], preferred_element_type=jnp.float32)
        share = grad.shape[0] // ctx_count
        for c in range(ctx_count):
            blocks[c, e] = grad[c * share : (c + 1) * share]
    for step in range(ctx_count):
        outs[step][...] = blocks[place_at(place, ctx_count, step)]
    feat, ex = lax.axis_index("feat"), lax.axis_index("ex")
    per_ex = own * feat_count
    for k, steps in enumerate(itertools.product(range(feat_count), range(ex_count))):
        from_feat, from_ex = place_at(feat, feat_count, steps[0], -1), place_at(ex, ex_count, steps[1], -1)
        for e in range(own):
            wanted = order[(from_feat * ex_count + from_ex) * own + e]
            rank = step_to(ex, lax.div(wanted, per_ex), ex_count) * per_ex + lax.rem(wanted, per_ex)
            ranks_ref[pl.ds(k * own + e, 1), :] = jnp.full((1, 128), rank, jnp.int32)
    copies[-1].wait()


def gradient(hidden, factor, cotangent, projection, lengths, order, counts):
    ctx_count, feat_count, ex_count = counts
    own, tokens, width = hidden.shape
    rank, model = factor.shape[0], cotangent.shape[2]
    shape = (own, rank // ctx_count, model)
    chunks = 4
    return pl.pallas_call(
        functools.partial(gradient_body, chunks, counts),
        out_shape=[jax.ShapeDtypeStruct(shape, jnp.float32)] * ctx_count
        + [
            jax.ShapeDtypeStruct((own * feat_count * ex_count, 128), jnp.int32),
            pltpu.VMEM(share_shape(projection, 0, ex_count), projection.dtype),
        ],
        in_specs=[HBM] * 4 + [pl.BlockSpec(memory_space=pltpu.SMEM), HBM],
        out_specs=[VMEM] * (ctx_count + 2),
        scratch_shapes=[
            pltpu.VMEM(hidden.shape, hidden.dtype),
            pltpu.VMEM(factor.shape, factor.dtype),
            pltpu.VMEM(cotangent.shape, cotangent.dtype),
            pltpu.VMEM((ctx_count,) + shape, jnp.float32),
            pltpu.SMEM(order.shape, order.dtype),
            pltpu.SemaphoreType.DMA((chunks + 3,)),
            pltpu.SemaphoreType.DMA,
        ],
        compiler_params=params(8),
    )(*map(hbm, (hidden, factor, cotangent, projection)), lengths, hbm(order))


def sum_body(*refs):
    total = refs[0][...]
    for ref in refs[1:-2]:
        total = total + ref[...]
    refs[-1][...] = total.astype(refs[-1].dtype)


def sum_rows(parts, dtype, after):
    return pl.pallas_call(
        sum_body,
        out_shape=jax.ShapeDtypeStruct(parts[0].shape, dtype),
        in_specs=[VMEM] * (len(parts) + 1),
        out_specs=VMEM,
        compiler_params=params(2),
    )(*parts, pltpu.with_memory_space_constraint(after, pltpu.VMEM))


def project_body(source_count, ranks_ref, projection_hbm, *refs):
    sources, shares, (out, last_share, rows_ref, sem) = refs[:source_count], refs[source_count:-4], refs[-4:]
    copy = share_copy(projection_hbm, last_share, sem, len(shares))
    copy.start()
    padded, width = out.shape
    own, share, model = sources[0].shape
    row = lax.broadcasted_iota(jnp.int32, (padded, model), 0)
    ranks = ranks_ref[...][:, :1]
    for r in range(share):
        rows = jnp.zeros((padded, model), jnp.float32)
        for k, source in enumerate(sources):
            for e in range(own):
                values = source[e, r : r + 1].astype(jnp.float32)
                rows = rows + jnp.where(row == ranks[k * own + e : k * own + e + 1], values, 0.0)
        rows_ref[:, r * model : (r + 1) * model] = rows.astype(jnp.bfloat16)
    for number, weights in enumerate((*shares, last_share)):
        first, depth = share_rows(projection_hbm.shape[0], number)
        if number == len(shares):
            copy.wait()
        part = jnp.dot(rows_ref[:, first : first + depth], weights[...], preferred_element_type=jnp.float32)
        if number == 0:
            out[...] = part
        else:
            out[...] += part


def project(sources, ranks, projection, shares, ex_count):
    depth, width = projection.shape
    padded = max(8, ranks.shape[0])
    return pl.pallas_call(
        functools.partial(project_body, len(sources)),
        out_shape=jax.ShapeDtypeStruct((padded, width // ex_count), jnp.float32),
        in_specs=[VMEM, HBM] + [VMEM] * (len(sources) + len(shares)),
        out_specs=VMEM,
        scratch_shapes=[
            pltpu.VMEM(share_shape(projection, len(shares), ex_count), projection.dtype),
            pltpu.VMEM((padded, depth), jnp.bfloat16),
            pltpu.SemaphoreType.DMA,
        ],
        compiler_params=params(8),
    )(ranks, hbm(projection), *sources, *[pltpu.with_memory_space_constraint(v, pltpu.VMEM) for v in shares])


def total_body(per_ex, ex_count, *refs):
    parts, outs = refs[: -2 * ex_count], refs[-2 * ex_count :]
    total = parts[0][...]
    for part in parts[1:]:
        total = total + part[...]
    squares = jnp.sum(total * total, axis=1, keepdims=True)
    for step in range(ex_count):
        rows = slice(step * per_ex, (step + 1) * per_ex)
        outs[2 * step][...] = total[rows]
        outs[2 * step + 1][...] = jnp.broadcast_to(squares[rows], (per_ex, 128))


def totals(parts, count, ex_count):
    per_ex, width = count // ex_count, parts[0].shape[1]
    shapes = [jax.ShapeDtypeStruct((per_ex, width), jnp.float32), jax.ShapeDtypeStruct((per_ex, 128), jnp.float32)]
    return pl.pallas_call(
        functools.partial(total_body, per_ex, ex_count),
        out_shape=shapes * ex_count,
        in_specs=[VMEM] * len(parts),
        out_specs=[VMEM] * (2 * ex_count),
        compiler_params=params(8),
    )(*parts)


def scale_body(ex_count, columns, *refs):
    rows, squares, out = refs[:ex_count], refs[ex_count:-1], refs[-1]
    width = rows[0].shape[1]
    total = squares[0][...]
    for square in squares[1:]:
        total = total + square[...]
    norm = jnp.sqrt(total[:, :1] / columns + 1e-06)
    for step in range(ex_count):
        place = place_at(lax.axis_index("ex"), ex_count, step, -1)
        out[:, pl.ds(pl.multiple_of(place * width, 128), width)] = rows[step][...] / norm


def scale(rows, squares, columns):
    per_ex, width = rows[0].shape
    return pl.pallas_call(
        functools.partial(scale_body, len(rows), columns),
        out_shape=jax.ShapeDtypeStruct((per_ex, width * len(rows)), jnp.float32),
        in_specs=[VMEM] * (len(rows) + len(squares)),
        out_specs=VMEM,
        compiler_params=params(8),
    )(*rows, *squares)


def per_device(hidden, cotangent, adapter_down_factor, projection, lengths, slot_example_order):
    counts = ctx_count, feat_count, ex_count = tuple(map(lax.axis_size, ("ctx", "feat", "ex")))
    count = hidden.shape[0] * feat_count * ex_count
    ctx_steps = range(1, ctx_count)
    chip_steps = list(itertools.product(range(feat_count), range(ex_count)))[1:]

    *blocks, ranks, share = gradient(
        hidden, adapter_down_factor.T, cotangent, projection, lengths, slot_example_order, counts
    )
    shares = [share, load(projection, 1, ex_count, ranks)]
    grad_rows = sum_rows(
        [blocks[0]] + [swap(blocks[s], ("ctx",), (s,)) for s in ctx_steps], jnp.bfloat16, shares[1]
    )
    shares.append(load(projection, 2, ex_count, grad_rows))
    sources = [grad_rows] + [swap(grad_rows, ("feat", "ex"), steps) for steps in chip_steps]
    product = project(sources, ranks, projection, shares, ex_count)
    outs = totals([product] + [swap(product, ("ctx",), (s,)) for s in ctx_steps], count, ex_count)
    rows = [outs[0]] + [swap(outs[2 * s], ("ex",), (s,)) for s in range(1, ex_count)]
    squares = [outs[1]] + [swap(outs[2 * s[1] + 1], ("feat", "ex"), s) for s in chip_steps]
    return scale(rows, squares, projection.shape[1] * feat_count)


def solution(mesh):
    in_specs = (
        P(("group", "feat", "ex"), "ctx", None),
        P(("group", "feat", "ex"), "ctx", None),
        P(),
        P("ctx", "feat"),
        P(("group", "feat", "ex")),
        P("group"),
    )
    out_specs = P(("group", "ex"), "feat")
    return jax.shard_map(
        per_device, mesh=mesh, in_specs=in_specs, out_specs=out_specs, check_vma=False
    )
```

```python
import functools
import itertools

import jax
import jax.numpy as jnp
from jax import lax
from jax.experimental import pallas as pl
from jax.experimental.pallas import tpu as pltpu
from jax.sharding import PartitionSpec as P

MIB = 1 << 20
SHARES = (1, 3, 2, 2)
VMEM = pl.BlockSpec(memory_space=pltpu.VMEM)
HBM = pl.BlockSpec(memory_space=pltpu.HBM)


def is_power(count):
    return count & (count - 1) == 0


def place_at(index, count, step, sign=1):
    if is_power(count):
        return index ^ step
    return (index + sign * step + count) % count


def step_to(index, target, count):
    if is_power(count):
        return index ^ target
    return lax.rem(target - index + count, count)


def exchange_steps(feat_count, ex_count):
    steps = itertools.product(range(feat_count), range(ex_count))
    return sorted(steps, key=lambda s: (any(s), not all(s), s))


def swap(value, axes, steps):
    sizes = [lax.axis_size(a) for a in axes]
    flat = lambda place: functools.reduce(lambda total, p: total * p[1] + p[0], zip(place, sizes), 0)
    pairs = [
        (flat(place), flat([place_at(i, n, s) for i, n, s in zip(place, sizes, steps)]))
        for place in itertools.product(*map(range, sizes))
    ]
    return lax.ppermute(value, tuple(axes) if len(axes) > 1 else axes[0], pairs)


def params(mib, **more):
    return pltpu.CompilerParams(vmem_limit_bytes=mib * MIB, **more)


def lane_dot(a, b):
    return lax.dot_general(a, b, (((1,), (1,)), ((), ())), preferred_element_type=jnp.float32)


def hbm(value):
    return pltpu.with_memory_space_constraint(value, pltpu.HBM)


def share_rows(depth, number):
    eighth = depth // sum(SHARES)
    return sum(SHARES[:number]) * eighth, SHARES[number] * eighth


def share_copy(projection_hbm, buffer, sem, number):
    first, rows = share_rows(projection_hbm.shape[0], number)
    width = buffer.shape[1]
    columns = pl.ds(pl.multiple_of(lax.axis_index("ex") * width, 128), width)
    return pltpu.make_async_copy(projection_hbm.at[pl.ds(first, rows), columns], buffer, sem)


def share_shape(projection, number, ex_count):
    depth, width = projection.shape
    return share_rows(depth, number)[1], width // ex_count


def load_body(number, after_ref, projection_hbm, buffer, sem):
    copy = share_copy(projection_hbm, buffer, sem, number)
    copy.start()
    copy.wait()


def load(projection, number, ex_count, after):
    return pl.pallas_call(
        functools.partial(load_body, number),
        out_shape=pltpu.VMEM(share_shape(projection, number, ex_count), projection.dtype),
        in_specs=[VMEM, HBM],
        out_specs=VMEM,
        scratch_shapes=[pltpu.SemaphoreType.DMA],
        compiler_params=params(2),
    )(after, hbm(projection))


def gradient_body(chunks, counts, hidden_hbm, factor_hbm, cotangent_hbm, projection_hbm, lengths, order_hbm, *refs):
    ctx_count, feat_count, ex_count = counts
    outs, ranks_ref, share_ref = refs[:ctx_count], refs[ctx_count], refs[ctx_count + 1]
    hidden, factor, cotangent, blocks, order, sems, order_sem = refs[ctx_count + 2 :]
    own, tokens, width = hidden.shape
    part = width // chunks
    order_copy = pltpu.make_async_copy(order_hbm, order, order_sem)
    order_copy.start()
    copies = [pltpu.make_async_copy(factor_hbm, factor, sems.at[0])]
    for k in range(chunks):
        columns = pl.ds(k * part, part)
        copies.append(
            pltpu.make_async_copy(hidden_hbm.at[:, :, columns], hidden.at[:, :, columns], sems.at[1 + k])
        )
    copies.append(pltpu.make_async_copy(cotangent_hbm, cotangent, sems.at[1 + chunks]))
    copies.append(share_copy(projection_hbm, share_ref, sems.at[2 + chunks], 0))
    for copy in copies:
        copy.start()
    copies[0].wait()
    down = [None] * own
    for k in range(chunks):
        copies[1 + k].wait()
        for e in range(own):
            product = lane_dot(factor[:, k * part : (k + 1) * part], hidden[e, :, k * part : (k + 1) * part])
            down[e] = product if k == 0 else down[e] + product
    copies[-2].wait()
    order_copy.wait()
    place = lax.axis_index("ctx")
    for e in range(own):
        rows = down[e].astype(jnp.bfloat16)
        position = place * tokens + lax.broadcasted_iota(jnp.int32, rows.shape, 1)
        rows = jnp.where(position < lengths[e], rows.astype(jnp.float32), 0.0).astype(jnp.bfloat16)
        grad = jnp.dot(rows, cotangent[e], preferred_element_type=jnp.float32)
        share = grad.shape[0] // ctx_count
        for c in range(ctx_count):
            blocks[c, e] = grad[c * share : (c + 1) * share]
    for step in range(ctx_count):
        outs[step][...] = blocks[place_at(place, ctx_count, step)]
    feat, ex = lax.axis_index("feat"), lax.axis_index("ex")
    per_ex = own * feat_count
    for k, steps in enumerate(exchange_steps(feat_count, ex_count)):
        from_feat, from_ex = place_at(feat, feat_count, steps[0], -1), place_at(ex, ex_count, steps[1], -1)
        for e in range(own):
            wanted = order[(from_feat * ex_count + from_ex) * own + e]
            rank = step_to(ex, lax.div(wanted, per_ex), ex_count) * per_ex + lax.rem(wanted, per_ex)
            ranks_ref[pl.ds(k * own + e, 1), :] = jnp.full((1, 128), rank, jnp.int32)
    copies[-1].wait()


def gradient(hidden, factor, cotangent, projection, lengths, order, counts):
    ctx_count, feat_count, ex_count = counts
    own, tokens, width = hidden.shape
    rank, model = factor.shape[0], cotangent.shape[2]
    shape = (own, rank // ctx_count, model)
    chunks = 2
    return pl.pallas_call(
        functools.partial(gradient_body, chunks, counts),
        out_shape=[jax.ShapeDtypeStruct(shape, jnp.float32)] * ctx_count
        + [
            jax.ShapeDtypeStruct((own * feat_count * ex_count, 128), jnp.int32),
            pltpu.VMEM(share_shape(projection, 0, ex_count), projection.dtype),
        ],
        in_specs=[HBM] * 4 + [pl.BlockSpec(memory_space=pltpu.SMEM), HBM],
        out_specs=[VMEM] * (ctx_count + 2),
        scratch_shapes=[
            pltpu.VMEM(hidden.shape, hidden.dtype),
            pltpu.VMEM(factor.shape, factor.dtype),
            pltpu.VMEM(cotangent.shape, cotangent.dtype),
            pltpu.VMEM((ctx_count,) + shape, jnp.float32),
            pltpu.SMEM(order.shape, order.dtype),
            pltpu.SemaphoreType.DMA((chunks + 3,)),
            pltpu.SemaphoreType.DMA,
        ],
        compiler_params=params(8),
    )(*map(hbm, (hidden, factor, cotangent, projection)), lengths, hbm(order))


def sum_body(*refs):
    total = refs[0][...]
    for ref in refs[1:-2]:
        total = total + ref[...]
    refs[-1][...] = total.astype(refs[-1].dtype)


def sum_rows(parts, dtype, after):
    return pl.pallas_call(
        sum_body,
        out_shape=jax.ShapeDtypeStruct(parts[0].shape, dtype),
        in_specs=[VMEM] * (len(parts) + 1),
        out_specs=VMEM,
        compiler_params=params(2),
    )(*parts, pltpu.with_memory_space_constraint(after, pltpu.VMEM))


def project_body(source_count, ranks_ref, projection_hbm, *refs):
    sources, shares, (out, last_share, rows_ref, sem) = refs[:source_count], refs[source_count:-4], refs[-4:]
    copy = share_copy(projection_hbm, last_share, sem, len(shares))
    copy.start()
    padded, count = rows_ref.shape[0], out.shape[0]
    own, share, model = sources[0].shape
    row = lax.broadcasted_iota(jnp.int32, (padded, model), 0)
    ranks = ranks_ref[...][:, :1]
    for r in range(share):
        rows = jnp.zeros((padded, model), jnp.float32)
        for k, source in enumerate(sources):
            for e in range(own):
                values = source[e, r : r + 1].astype(jnp.float32)
                rows = rows + jnp.where(row == ranks[k * own + e : k * own + e + 1], values, 0.0)
        rows_ref[:, r * model : (r + 1) * model] = rows.astype(jnp.bfloat16)
    for number, weights in enumerate((*shares, last_share)):
        first, depth = share_rows(projection_hbm.shape[0], number)
        if number == len(shares):
            copy.wait()
        part = jnp.dot(rows_ref[:, first : first + depth], weights[...], preferred_element_type=jnp.float32)
        total = part if number == 0 else total + part
    out[...] = total[:count]


def project(sources, ranks, projection, shares, ex_count):
    depth, width = projection.shape
    count = ranks.shape[0]
    padded = max(8, count)
    return pl.pallas_call(
        functools.partial(project_body, len(sources)),
        out_shape=jax.ShapeDtypeStruct((count, width // ex_count), jnp.float32),
        in_specs=[VMEM, HBM] + [VMEM] * (len(sources) + len(shares)),
        out_specs=VMEM,
        scratch_shapes=[
            pltpu.VMEM(share_shape(projection, len(shares), ex_count), projection.dtype),
            pltpu.VMEM((padded, depth), jnp.bfloat16),
            pltpu.SemaphoreType.DMA,
        ],
        compiler_params=params(8),
    )(ranks, hbm(projection), *sources, *[pltpu.with_memory_space_constraint(v, pltpu.VMEM) for v in shares])


def total_body(ex_count, *refs):
    parts, (own_rows, *others), squares_outs = refs[: -2 * ex_count], refs[-2 * ex_count : -ex_count], refs[-ex_count:]
    total = parts[0][...]
    for part in parts[1:]:
        total = total + part[...]
    squares = jnp.sum(total * total, axis=1, keepdims=True)
    per_ex, width = own_rows.shape
    own_rows[...] = total[:per_ex]
    for step in range(ex_count):
        rows = slice(step * per_ex, (step + 1) * per_ex)
        spread = jnp.broadcast_to(squares[rows], (per_ex, 128))
        squares_outs[step][...] = spread
        if step:
            others[step - 1][:, :width] = total[rows]
            others[step - 1][:, width:] = spread


def totals(parts, ex_count):
    count, width = parts[0].shape
    per_ex = count // ex_count
    shape = lambda columns: jax.ShapeDtypeStruct((per_ex, columns), jnp.float32)
    outs = pl.pallas_call(
        functools.partial(total_body, ex_count),
        out_shape=[shape(width)] + [shape(width + 128)] * (ex_count - 1) + [shape(128)] * ex_count,
        in_specs=[VMEM] * len(parts),
        out_specs=[VMEM] * (2 * ex_count),
        compiler_params=params(8),
    )(*parts)
    return outs[:ex_count], outs[ex_count:]


def scale_body(ex_count, columns, *refs):
    rows, squares, out = refs[:ex_count], refs[ex_count:-1], refs[-1]
    width = rows[0].shape[1]
    total = squares[0][...]
    for square in squares[1:]:
        total = total + square[...]
    for row in rows[1:]:
        total = total + row[:, width:]
    norm = jnp.sqrt(total[:, :1] / columns + 1e-06)
    for step in range(ex_count):
        place = place_at(lax.axis_index("ex"), ex_count, step, -1)
        out[:, pl.ds(pl.multiple_of(place * width, 128), width)] = rows[step][:, :width] / norm


def scale(rows, squares, columns):
    per_ex, width = rows[0].shape
    return pl.pallas_call(
        functools.partial(scale_body, len(rows), columns),
        out_shape=jax.ShapeDtypeStruct((per_ex, width * len(rows)), jnp.float32),
        in_specs=[VMEM] * (len(rows) + len(squares)),
        out_specs=VMEM,
        compiler_params=params(8),
    )(*rows, *squares)


def per_device(hidden, cotangent, adapter_down_factor, projection, lengths, slot_example_order):
    counts = ctx_count, feat_count, ex_count = tuple(map(lax.axis_size, ("ctx", "feat", "ex")))
    ctx_steps = range(1, ctx_count)
    chip_steps = exchange_steps(feat_count, ex_count)[1:]

    *blocks, ranks, share = gradient(
        hidden, adapter_down_factor.T, cotangent, projection, lengths, slot_example_order, counts
    )
    shares = [share, load(projection, 1, ex_count, ranks)]
    grad_rows = sum_rows(
        [blocks[0]] + [swap(blocks[s], ("ctx",), (s,)) for s in reversed(ctx_steps)], jnp.bfloat16, shares[1]
    )
    shares.append(load(projection, 2, ex_count, grad_rows))
    sources = [grad_rows] + [swap(grad_rows, ("feat", "ex"), s) for s in chip_steps]
    product = project(sources, ranks, projection, shares, ex_count)
    rows, squares = totals([product] + [swap(product, ("ctx",), (s,)) for s in ctx_steps], ex_count)
    taken = [rows[0]] + [swap(rows[s], ("ex",), (s,)) for s in range(1, ex_count)]
    sums = [squares[0]] + [swap(squares[e], ("feat", "ex"), (f, e)) for f, e in chip_steps if f]
    return scale(taken, sums, projection.shape[1] * feat_count)


def solution(mesh):
    in_specs = (
        P(("group", "feat", "ex"), "ctx", None),
        P(("group", "feat", "ex"), "ctx", None),
        P(),
        P("ctx", "feat"),
        P(("group", "feat", "ex")),
        P("group"),
    )
    out_specs = P(("group", "ex"), "feat")
    return jax.shard_map(
        per_device, mesh=mesh, in_specs=in_specs, out_specs=out_specs, check_vma=False
    )
```

```python
import functools
import itertools

import jax
import jax.numpy as jnp
from jax import lax
from jax.experimental import pallas as pl
from jax.experimental.pallas import tpu as pltpu
from jax.sharding import PartitionSpec as P

MIB = 1 << 20
SHARES = (1, 3, 2, 2)
VMEM = pl.BlockSpec(memory_space=pltpu.VMEM)
HBM = pl.BlockSpec(memory_space=pltpu.HBM)


def is_power(count):
    return count & (count - 1) == 0


def place_at(index, count, step, sign=1):
    if is_power(count):
        return index ^ step
    return (index + sign * step + count) % count


def step_to(index, target, count):
    if is_power(count):
        return index ^ target
    return lax.rem(target - index + count, count)


def exchange_steps(feat_count, ex_count):
    steps = itertools.product(range(feat_count), range(ex_count))
    return sorted(steps, key=lambda s: (any(s), not all(s), s))


def swap(value, axes, steps):
    sizes = [lax.axis_size(a) for a in axes]
    flat = lambda place: functools.reduce(lambda total, p: total * p[1] + p[0], zip(place, sizes), 0)
    pairs = [
        (flat(place), flat([place_at(i, n, s) for i, n, s in zip(place, sizes, steps)]))
        for place in itertools.product(*map(range, sizes))
    ]
    return lax.ppermute(value, tuple(axes) if len(axes) > 1 else axes[0], pairs)


def params(mib, **more):
    return pltpu.CompilerParams(vmem_limit_bytes=mib * MIB, **more)


def lane_dot(a, b):
    return lax.dot_general(a, b, (((1,), (1,)), ((), ())), preferred_element_type=jnp.float32)


def hbm(value):
    return pltpu.with_memory_space_constraint(value, pltpu.HBM)


def share_rows(depth, number):
    eighth = depth // sum(SHARES)
    return sum(SHARES[:number]) * eighth, SHARES[number] * eighth


def share_copy(projection_hbm, buffer, sem, number):
    first, rows = share_rows(projection_hbm.shape[0], number)
    width = buffer.shape[1]
    columns = pl.ds(pl.multiple_of(lax.axis_index("ex") * width, 128), width)
    return pltpu.make_async_copy(projection_hbm.at[pl.ds(first, rows), columns], buffer, sem)


def share_shape(projection, number, ex_count):
    depth, width = projection.shape
    return share_rows(depth, number)[1], width // ex_count


def load_body(number, after_ref, projection_hbm, buffer, sem):
    copy = share_copy(projection_hbm, buffer, sem, number)
    copy.start()
    copy.wait()


def load(projection, number, ex_count, after):
    return pl.pallas_call(
        functools.partial(load_body, number),
        out_shape=pltpu.VMEM(share_shape(projection, number, ex_count), projection.dtype),
        in_specs=[VMEM, HBM],
        out_specs=VMEM,
        scratch_shapes=[pltpu.SemaphoreType.DMA],
        compiler_params=params(2),
    )(after, hbm(projection))


def gradient_body(chunks, counts, hidden_hbm, factor_hbm, cotangent_hbm, projection_hbm, lengths, order_hbm, *refs):
    ctx_count, feat_count, ex_count = counts
    outs, ranks_ref, share_ref = refs[:ctx_count], refs[ctx_count], refs[ctx_count + 1]
    hidden, factor, cotangent, blocks, order, sems, order_sem = refs[ctx_count + 2 :]
    own, tokens, width = hidden.shape
    part = width // chunks
    order_copy = pltpu.make_async_copy(order_hbm, order, order_sem)
    order_copy.start()
    copies = [pltpu.make_async_copy(factor_hbm, factor, sems.at[0])]
    for k in range(chunks):
        columns = pl.ds(k * part, part)
        copies.append(
            pltpu.make_async_copy(hidden_hbm.at[:, :, columns], hidden.at[:, :, columns], sems.at[1 + k])
        )
    copies.append(pltpu.make_async_copy(cotangent_hbm, cotangent, sems.at[1 + chunks]))
    copies.append(share_copy(projection_hbm, share_ref, sems.at[2 + chunks], 0))
    for copy in copies:
        copy.start()
    copies[0].wait()
    down = [None] * own
    for k in range(chunks):
        copies[1 + k].wait()
        for e in range(own):
            product = lane_dot(factor[:, k * part : (k + 1) * part], hidden[e, :, k * part : (k + 1) * part])
            down[e] = product if k == 0 else down[e] + product
    copies[-2].wait()
    order_copy.wait()
    place = lax.axis_index("ctx")
    for e in range(own):
        rows = down[e].astype(jnp.bfloat16)
        position = place * tokens + lax.broadcasted_iota(jnp.int32, rows.shape, 1)
        rows = jnp.where(position < lengths[e], rows.astype(jnp.float32), 0.0).astype(jnp.bfloat16)
        grad = jnp.dot(rows, cotangent[e], preferred_element_type=jnp.float32)
        share = grad.shape[0] // ctx_count
        for c in range(ctx_count):
            blocks[c, e] = grad[c * share : (c + 1) * share]
    for step in range(ctx_count):
        outs[step][...] = blocks[place_at(place, ctx_count, step)]
    feat, ex = lax.axis_index("feat"), lax.axis_index("ex")
    per_ex = own * feat_count
    for k, steps in enumerate(exchange_steps(feat_count, ex_count)):
        from_feat, from_ex = place_at(feat, feat_count, steps[0], -1), place_at(ex, ex_count, steps[1], -1)
        for e in range(own):
            wanted = order[(from_feat * ex_count + from_ex) * own + e]
            rank = step_to(ex, lax.div(wanted, per_ex), ex_count) * per_ex + lax.rem(wanted, per_ex)
            ranks_ref[pl.ds(k * own + e, 1), :] = jnp.full((1, 128), rank, jnp.int32)
    copies[-1].wait()


def gradient(hidden, factor, cotangent, projection, lengths, order, counts):
    ctx_count, feat_count, ex_count = counts
    own, tokens, width = hidden.shape
    rank, model = factor.shape[0], cotangent.shape[2]
    shape = (own, rank // ctx_count, model)
    chunks = 2
    return pl.pallas_call(
        functools.partial(gradient_body, chunks, counts),
        out_shape=[jax.ShapeDtypeStruct(shape, jnp.float32)] * ctx_count
        + [
            jax.ShapeDtypeStruct((own * feat_count * ex_count, 128), jnp.int32),
            pltpu.VMEM(share_shape(projection, 0, ex_count), projection.dtype),
        ],
        in_specs=[HBM] * 4 + [pl.BlockSpec(memory_space=pltpu.SMEM), HBM],
        out_specs=[VMEM] * (ctx_count + 2),
        scratch_shapes=[
            pltpu.VMEM(hidden.shape, hidden.dtype),
            pltpu.VMEM(factor.shape, factor.dtype),
            pltpu.VMEM(cotangent.shape, cotangent.dtype),
            pltpu.VMEM((ctx_count,) + shape, jnp.float32),
            pltpu.SMEM(order.shape, order.dtype),
            pltpu.SemaphoreType.DMA((chunks + 3,)),
            pltpu.SemaphoreType.DMA,
        ],
        compiler_params=params(8),
    )(*map(hbm, (hidden, factor, cotangent, projection)), lengths, hbm(order))


def sum_body(*refs):
    total = refs[0][...]
    for ref in refs[1:-2]:
        total = total + ref[...]
    refs[-1][...] = total.astype(refs[-1].dtype)


def sum_rows(parts, dtype, after):
    return pl.pallas_call(
        sum_body,
        out_shape=jax.ShapeDtypeStruct(parts[0].shape, dtype),
        in_specs=[VMEM] * (len(parts) + 1),
        out_specs=VMEM,
        compiler_params=params(2),
    )(*parts, pltpu.with_memory_space_constraint(after, pltpu.VMEM))


def project_body(source_count, ranks_ref, projection_hbm, *refs):
    sources, shares, (out, last_share, rows_ref, sem) = refs[:source_count], refs[source_count:-4], refs[-4:]
    copy = share_copy(projection_hbm, last_share, sem, len(shares))
    copy.start()
    padded, count = rows_ref.shape[0], out.shape[0]
    own, share, model = sources[0].shape
    row = lax.broadcasted_iota(jnp.int32, (padded, model), 0)
    ranks = ranks_ref[...][:, :1]
    for r in range(share):
        rows = jnp.zeros((padded, model), jnp.float32)
        for k, source in enumerate(sources):
            for e in range(own):
                values = source[e, r : r + 1].astype(jnp.float32)
                rows = rows + jnp.where(row == ranks[k * own + e : k * own + e + 1], values, 0.0)
        rows_ref[:, r * model : (r + 1) * model] = rows.astype(jnp.bfloat16)
    for number, weights in enumerate((*shares, last_share)):
        first, depth = share_rows(projection_hbm.shape[0], number)
        if number == len(shares):
            copy.wait()
        part = jnp.dot(rows_ref[:, first : first + depth], weights[...], preferred_element_type=jnp.float32)
        total = part if number == 0 else total + part
    out[...] = total[:count]


def project(sources, ranks, projection, shares, ex_count):
    depth, width = projection.shape
    count = ranks.shape[0]
    padded = max(8, count)
    return pl.pallas_call(
        functools.partial(project_body, len(sources)),
        out_shape=jax.ShapeDtypeStruct((count, width // ex_count), jnp.float32),
        in_specs=[VMEM, HBM] + [VMEM] * (len(sources) + len(shares)),
        out_specs=VMEM,
        scratch_shapes=[
            pltpu.VMEM(share_shape(projection, len(shares), ex_count), projection.dtype),
            pltpu.VMEM((padded, depth), jnp.bfloat16),
            pltpu.SemaphoreType.DMA,
        ],
        compiler_params=params(8),
    )(ranks, hbm(projection), *sources, *[pltpu.with_memory_space_constraint(v, pltpu.VMEM) for v in shares])


def total_body(ex_count, *refs):
    parts = refs[: -2 * ex_count - 1]
    near, *others, own_rows, own_squares = refs[-2 * ex_count - 1 :]
    total = parts[0][...]
    for part in parts[1:]:
        total = total + part[...]
    squares = jnp.sum(total * total, axis=1, keepdims=True)
    per_ex, width = own_rows.shape
    own_rows[...] = total[:per_ex]
    for step in range(ex_count):
        rows = slice(step * per_ex, (step + 1) * per_ex)
        spread = jnp.broadcast_to(squares[rows], (per_ex, 128))
        if step == 0:
            near[...] = spread
            own_squares[...] = spread
        else:
            others[2 * step - 2][:, :width] = total[rows]
            others[2 * step - 2][:, width:] = spread
            others[2 * step - 1][...] = spread


def totals(parts, ex_count):
    count, width = parts[0].shape
    per_ex = count // ex_count
    shape = lambda columns: jax.ShapeDtypeStruct((per_ex, columns), jnp.float32)
    near, *others, own_rows, own_squares = pl.pallas_call(
        functools.partial(total_body, ex_count),
        out_shape=[shape(128)] + [shape(width + 128), shape(128)] * (ex_count - 1) + [shape(width), shape(128)],
        in_specs=[VMEM] * len(parts),
        out_specs=[VMEM] * (2 * ex_count + 1),
        compiler_params=params(8),
    )(*parts)
    return [own_rows, *others[::2]], [near, *others[1::2]], own_squares


def scale_body(near_count, ex_count, columns, *refs):
    rows, squares, out = refs[near_count : near_count + ex_count], refs[:near_count] + refs[near_count + ex_count : -1], refs[-1]
    width = rows[0].shape[1]
    total = squares[0][...]
    for square in squares[1:]:
        total = total + square[...]
    for row in rows[1:]:
        total = total + row[:, width:]
    norm = jnp.sqrt(total[:, :1] / columns + 1e-06)
    for step in range(ex_count):
        place = place_at(lax.axis_index("ex"), ex_count, step, -1)
        out[:, pl.ds(pl.multiple_of(place * width, 128), width)] = rows[step][:, :width] / norm


def scale(near, rows, squares, columns):
    per_ex, width = rows[0].shape
    operands = (*near, *rows, *squares)
    return pl.pallas_call(
        functools.partial(scale_body, len(near), len(rows), columns),
        out_shape=jax.ShapeDtypeStruct((per_ex, width * len(rows)), jnp.float32),
        in_specs=[VMEM] * len(operands),
        out_specs=VMEM,
        compiler_params=params(8),
    )(*operands)


def per_device(hidden, cotangent, adapter_down_factor, projection, lengths, slot_example_order):
    counts = ctx_count, feat_count, ex_count = tuple(map(lax.axis_size, ("ctx", "feat", "ex")))
    ctx_steps = sorted(range(1, ctx_count), key=lambda s: (s == 1, s))
    chip_steps = exchange_steps(feat_count, ex_count)[1:]

    *blocks, ranks, share = gradient(
        hidden, adapter_down_factor.T, cotangent, projection, lengths, slot_example_order, counts
    )
    shares = [share, load(projection, 1, ex_count, ranks)]
    grad_rows = sum_rows(
        [blocks[0]] + [swap(blocks[s], ("ctx",), (s,)) for s in ctx_steps], jnp.bfloat16, shares[1]
    )
    shares.append(load(projection, 2, ex_count, grad_rows))
    sources = [grad_rows] + [swap(grad_rows, ("feat", "ex"), s) for s in chip_steps]
    product = project(sources, ranks, projection, shares, ex_count)
    rows, squares, own_squares = totals([product] + [swap(product, ("ctx",), (s,)) for s in reversed(ctx_steps)], ex_count)
    taken = [rows[0]] + [swap(rows[s], ("ex",), (s,)) for s in range(1, ex_count)]
    near, far = (
        [swap(squares[e], ("feat", "ex"), (f, e)) for f, e in chip_steps if f and bool(e) == both] for both in (False, True)
    )
    return scale(near, taken, [*far, own_squares], projection.shape[1] * feat_count)


def solution(mesh):
    in_specs = (
        P(("group", "feat", "ex"), "ctx", None),
        P(("group", "feat", "ex"), "ctx", None),
        P(),
        P("ctx", "feat"),
        P(("group", "feat", "ex")),
        P("group"),
    )
    out_specs = P(("group", "ex"), "feat")
    return jax.shard_map(
        per_device, mesh=mesh, in_specs=in_specs, out_specs=out_specs, check_vma=False
    )
```

```python
import functools
import itertools

import jax
import jax.numpy as jnp
from jax import lax
from jax.experimental import pallas as pl
from jax.experimental.pallas import tpu as pltpu
from jax.sharding import PartitionSpec as P

MIB = 1 << 20
SHARES = (1, 3, 3, 1)
VMEM = pl.BlockSpec(memory_space=pltpu.VMEM)
HBM = pl.BlockSpec(memory_space=pltpu.HBM)


def is_power(count):
    return count & (count - 1) == 0


def place_at(index, count, step, sign=1):
    if is_power(count):
        return index ^ step
    return (index + sign * step + count) % count


def step_to(index, target, count):
    if is_power(count):
        return index ^ target
    return lax.rem(target - index + count, count)


def exchange_steps(feat_count, ex_count):
    steps = itertools.product(range(feat_count), range(ex_count))
    return sorted(steps, key=lambda s: (any(s), not all(s), s))


def swap(value, axes, steps):
    sizes = [lax.axis_size(a) for a in axes]
    flat = lambda place: functools.reduce(lambda total, p: total * p[1] + p[0], zip(place, sizes), 0)
    pairs = [
        (flat(place), flat([place_at(i, n, s) for i, n, s in zip(place, sizes, steps)]))
        for place in itertools.product(*map(range, sizes))
    ]
    return lax.ppermute(value, tuple(axes) if len(axes) > 1 else axes[0], pairs)


def params(mib, **more):
    return pltpu.CompilerParams(vmem_limit_bytes=mib * MIB, **more)


def lane_dot(a, b):
    return lax.dot_general(a, b, (((1,), (1,)), ((), ())), preferred_element_type=jnp.float32)


def hbm(value):
    return pltpu.with_memory_space_constraint(value, pltpu.HBM)


def share_rows(depth, number):
    eighth = depth // sum(SHARES)
    return sum(SHARES[:number]) * eighth, SHARES[number] * eighth


def share_copy(projection_hbm, buffer, sem, number):
    first, rows = share_rows(projection_hbm.shape[0], number)
    width = buffer.shape[1]
    columns = pl.ds(pl.multiple_of(lax.axis_index("ex") * width, 128), width)
    return pltpu.make_async_copy(projection_hbm.at[pl.ds(first, rows), columns], buffer, sem)


def share_shape(projection, number, ex_count):
    depth, width = projection.shape
    return share_rows(depth, number)[1], width // ex_count


def load_body(number, after_ref, projection_hbm, buffer, sem):
    copy = share_copy(projection_hbm, buffer, sem, number)
    copy.start()
    copy.wait()


def load(projection, number, ex_count, after):
    return pl.pallas_call(
        functools.partial(load_body, number),
        out_shape=pltpu.VMEM(share_shape(projection, number, ex_count), projection.dtype),
        in_specs=[VMEM, HBM],
        out_specs=VMEM,
        scratch_shapes=[pltpu.SemaphoreType.DMA],
        compiler_params=params(2),
    )(after, hbm(projection))


def gradient_body(chunks, counts, hidden_hbm, factor_hbm, cotangent_hbm, projection_hbm, lengths, order_hbm, *refs):
    ctx_count, feat_count, ex_count = counts
    outs, ranks_ref, share_ref = refs[:ctx_count], refs[ctx_count], refs[ctx_count + 1]
    hidden, factor, cotangent, blocks, order, sems, order_sem = refs[ctx_count + 2 :]
    own, tokens, width = hidden.shape
    part = width // chunks
    order_copy = pltpu.make_async_copy(order_hbm, order, order_sem)
    order_copy.start()
    copies = [pltpu.make_async_copy(factor_hbm, factor, sems.at[0])]
    for k in range(chunks):
        columns = pl.ds(k * part, part)
        copies.append(
            pltpu.make_async_copy(hidden_hbm.at[:, :, columns], hidden.at[:, :, columns], sems.at[1 + k])
        )
    copies.append(pltpu.make_async_copy(cotangent_hbm, cotangent, sems.at[1 + chunks]))
    copies.append(share_copy(projection_hbm, share_ref, sems.at[2 + chunks], 0))
    for copy in copies:
        copy.start()
    copies[0].wait()
    down = [None] * own
    for k in range(chunks):
        copies[1 + k].wait()
        for e in range(own):
            product = lane_dot(factor[:, k * part : (k + 1) * part], hidden[e, :, k * part : (k + 1) * part])
            down[e] = product if k == 0 else down[e] + product
    copies[-2].wait()
    order_copy.wait()
    place = lax.axis_index("ctx")
    for e in range(own):
        rows = down[e].astype(jnp.bfloat16)
        position = place * tokens + lax.broadcasted_iota(jnp.int32, rows.shape, 1)
        rows = jnp.where(position < lengths[e], rows.astype(jnp.float32), 0.0).astype(jnp.bfloat16)
        grad = jnp.dot(rows, cotangent[e], preferred_element_type=jnp.float32)
        share = grad.shape[0] // ctx_count
        for c in range(ctx_count):
            blocks[c, e] = grad[c * share : (c + 1) * share]
    for step in range(ctx_count):
        outs[step][...] = blocks[place_at(place, ctx_count, step)]
    feat, ex = lax.axis_index("feat"), lax.axis_index("ex")
    per_ex = own * feat_count
    for k, steps in enumerate(exchange_steps(feat_count, ex_count)):
        from_feat, from_ex = place_at(feat, feat_count, steps[0], -1), place_at(ex, ex_count, steps[1], -1)
        for e in range(own):
            wanted = order[(from_feat * ex_count + from_ex) * own + e]
            rank = step_to(ex, lax.div(wanted, per_ex), ex_count) * per_ex + lax.rem(wanted, per_ex)
            ranks_ref[pl.ds(k * own + e, 1), :] = jnp.full((1, 128), rank, jnp.int32)
    copies[-1].wait()


def gradient(hidden, factor, cotangent, projection, lengths, order, counts):
    ctx_count, feat_count, ex_count = counts
    own, tokens, width = hidden.shape
    rank, model = factor.shape[0], cotangent.shape[2]
    shape = (own, rank // ctx_count, model)
    chunks = 2
    return pl.pallas_call(
        functools.partial(gradient_body, chunks, counts),
        out_shape=[jax.ShapeDtypeStruct(shape, jnp.float32)] * ctx_count
        + [
            jax.ShapeDtypeStruct((own * feat_count * ex_count, 128), jnp.int32),
            pltpu.VMEM(share_shape(projection, 0, ex_count), projection.dtype),
        ],
        in_specs=[HBM] * 4 + [pl.BlockSpec(memory_space=pltpu.SMEM), HBM],
        out_specs=[VMEM] * (ctx_count + 2),
        scratch_shapes=[
            pltpu.VMEM(hidden.shape, hidden.dtype),
            pltpu.VMEM(factor.shape, factor.dtype),
            pltpu.VMEM(cotangent.shape, cotangent.dtype),
            pltpu.VMEM((ctx_count,) + shape, jnp.float32),
            pltpu.SMEM(order.shape, order.dtype),
            pltpu.SemaphoreType.DMA((chunks + 3,)),
            pltpu.SemaphoreType.DMA,
        ],
        compiler_params=params(8),
    )(*map(hbm, (hidden, factor, cotangent, projection)), lengths, hbm(order))


def sum_body(*refs):
    total = refs[0][...]
    for ref in refs[1:-2]:
        total = total + ref[...]
    refs[-1][...] = total.astype(refs[-1].dtype)


def sum_rows(parts, dtype, after):
    return pl.pallas_call(
        sum_body,
        out_shape=jax.ShapeDtypeStruct(parts[0].shape, dtype),
        in_specs=[VMEM] * (len(parts) + 1),
        out_specs=VMEM,
        compiler_params=params(2),
    )(*parts, pltpu.with_memory_space_constraint(after, pltpu.VMEM))


def project_body(source_count, ranks_ref, projection_hbm, *refs):
    sources, shares, (out, last_share, rows_ref, sem) = refs[:source_count], refs[source_count:-4], refs[-4:]
    copy = share_copy(projection_hbm, last_share, sem, len(shares))
    copy.start()
    padded, count = rows_ref.shape[0], out.shape[0]
    own, share, model = sources[0].shape
    row = lax.broadcasted_iota(jnp.int32, (padded, model), 0)
    ranks = ranks_ref[...][:, :1]
    for r in range(share):
        rows = jnp.zeros((padded, model), jnp.float32)
        for k, source in enumerate(sources):
            for e in range(own):
                values = source[e, r : r + 1].astype(jnp.float32)
                rows = rows + jnp.where(row == ranks[k * own + e : k * own + e + 1], values, 0.0)
        rows_ref[:, r * model : (r + 1) * model] = rows.astype(jnp.bfloat16)
    for number, weights in enumerate((*shares, last_share)):
        first, depth = share_rows(projection_hbm.shape[0], number)
        if number == len(shares):
            copy.wait()
        part = jnp.dot(rows_ref[:, first : first + depth], weights[...], preferred_element_type=jnp.float32)
        total = part if number == 0 else total + part
    out[...] = total[:count]


def project(sources, ranks, projection, shares, ex_count):
    depth, width = projection.shape
    count = ranks.shape[0]
    padded = max(8, count)
    return pl.pallas_call(
        functools.partial(project_body, len(sources)),
        out_shape=jax.ShapeDtypeStruct((count, width // ex_count), jnp.float32),
        in_specs=[VMEM, HBM] + [VMEM] * (len(sources) + len(shares)),
        out_specs=VMEM,
        scratch_shapes=[
            pltpu.VMEM(share_shape(projection, len(shares), ex_count), projection.dtype),
            pltpu.VMEM((padded, depth), jnp.bfloat16),
            pltpu.SemaphoreType.DMA,
        ],
        compiler_params=params(8),
    )(ranks, hbm(projection), *sources, *[pltpu.with_memory_space_constraint(v, pltpu.VMEM) for v in shares])


def total_body(ex_count, *refs):
    parts = refs[: -2 * ex_count - 1]
    near, *others, own_rows, own_squares = refs[-2 * ex_count - 1 :]
    total = parts[0][...]
    for part in parts[1:]:
        total = total + part[...]
    squares = jnp.sum(total * total, axis=1, keepdims=True)
    per_ex, width = own_rows.shape
    own_rows[...] = total[:per_ex]
    for step in range(ex_count):
        rows = slice(step * per_ex, (step + 1) * per_ex)
        spread = jnp.broadcast_to(squares[rows], (per_ex, 128))
        if step == 0:
            near[...] = spread
            own_squares[...] = spread
        else:
            others[2 * step - 2][:, :width] = total[rows]
            others[2 * step - 2][:, width:] = spread
            others[2 * step - 1][...] = spread


def totals(parts, ex_count):
    count, width = parts[0].shape
    per_ex = count // ex_count
    shape = lambda columns: jax.ShapeDtypeStruct((per_ex, columns), jnp.float32)
    near, *others, own_rows, own_squares = pl.pallas_call(
        functools.partial(total_body, ex_count),
        out_shape=[shape(128)] + [shape(width + 128), shape(128)] * (ex_count - 1) + [shape(width), shape(128)],
        in_specs=[VMEM] * len(parts),
        out_specs=[VMEM] * (2 * ex_count + 1),
        compiler_params=params(8),
    )(*parts)
    return [own_rows, *others[::2]], [near, *others[1::2]], own_squares


def scale_body(near_count, ex_count, columns, *refs):
    rows, squares, out = refs[near_count : near_count + ex_count], refs[:near_count] + refs[near_count + ex_count : -1], refs[-1]
    width = rows[0].shape[1]
    total = squares[0][...]
    for square in squares[1:]:
        total = total + square[...]
    for row in rows[1:]:
        total = total + row[:, width:]
    norm = jnp.sqrt(total[:, :1] / columns + 1e-06)
    for step in range(ex_count):
        place = place_at(lax.axis_index("ex"), ex_count, step, -1)
        out[:, pl.ds(pl.multiple_of(place * width, 128), width)] = rows[step][:, :width] / norm


def scale(near, rows, squares, columns):
    per_ex, width = rows[0].shape
    operands = (*near, *rows, *squares)
    return pl.pallas_call(
        functools.partial(scale_body, len(near), len(rows), columns),
        out_shape=jax.ShapeDtypeStruct((per_ex, width * len(rows)), jnp.float32),
        in_specs=[VMEM] * len(operands),
        out_specs=VMEM,
        compiler_params=params(8),
    )(*operands)


def per_device(hidden, cotangent, adapter_down_factor, projection, lengths, slot_example_order):
    counts = ctx_count, feat_count, ex_count = tuple(map(lax.axis_size, ("ctx", "feat", "ex")))
    ctx_steps = sorted(range(1, ctx_count), key=lambda s: (s == 1, s))
    chip_steps = exchange_steps(feat_count, ex_count)[1:]

    *blocks, ranks, share = gradient(
        hidden, adapter_down_factor.T, cotangent, projection, lengths, slot_example_order, counts
    )
    shares = [share, load(projection, 1, ex_count, ranks)]
    grad_rows = sum_rows(
        [blocks[0]] + [swap(blocks[s], ("ctx",), (s,)) for s in ctx_steps], jnp.bfloat16, shares[1]
    )
    shares.append(load(projection, 2, ex_count, grad_rows))
    sources = [grad_rows] + [swap(grad_rows, ("feat", "ex"), s) for s in chip_steps]
    product = project(sources, ranks, projection, shares, ex_count)
    rows, squares, own_squares = totals([product] + [swap(product, ("ctx",), (s,)) for s in reversed(ctx_steps)], ex_count)
    taken = [rows[0]] + [swap(rows[s], ("ex",), (s,)) for s in range(1, ex_count)]
    near, far = (
        [swap(squares[e], ("feat", "ex"), (f, e)) for f, e in chip_steps if f and bool(e) == both] for both in (False, True)
    )
    return scale(near, taken, [*far, own_squares], projection.shape[1] * feat_count)


def solution(mesh):
    in_specs = (
        P(("group", "feat", "ex"), "ctx", None),
        P(("group", "feat", "ex"), "ctx", None),
        P(),
        P("ctx", "feat"),
        P(("group", "feat", "ex")),
        P("group"),
    )
    out_specs = P(("group", "ex"), "feat")
    return jax.shard_map(
        per_device, mesh=mesh, in_specs=in_specs, out_specs=out_specs, check_vma=False
    )
```

```python
import functools
import itertools

import jax
import jax.numpy as jnp
from jax import lax
from jax.experimental import pallas as pl
from jax.experimental.pallas import tpu as pltpu
from jax.sharding import PartitionSpec as P

MIB = 1 << 20
SHARES = (1, 3, 3, 1)
VMEM = pl.BlockSpec(memory_space=pltpu.VMEM)
HBM = pl.BlockSpec(memory_space=pltpu.HBM)


def is_power(count):
    return count & (count - 1) == 0


def place_at(index, count, step, sign=1):
    if is_power(count):
        return index ^ step
    return (index + sign * step + count) % count


def step_to(index, target, count):
    if is_power(count):
        return index ^ target
    return lax.rem(target - index + count, count)


def exchange_steps(feat_count, ex_count):
    steps = itertools.product(range(feat_count), range(ex_count))
    return sorted(steps, key=lambda s: (any(s), not all(s), s))


def swap(value, axes, steps):
    sizes = [lax.axis_size(a) for a in axes]
    flat = lambda place: functools.reduce(lambda total, p: total * p[1] + p[0], zip(place, sizes), 0)
    pairs = [
        (flat(place), flat([place_at(i, n, s) for i, n, s in zip(place, sizes, steps)]))
        for place in itertools.product(*map(range, sizes))
    ]
    return lax.ppermute(value, tuple(axes) if len(axes) > 1 else axes[0], pairs)


def params(mib, **more):
    return pltpu.CompilerParams(vmem_limit_bytes=mib * MIB, **more)


def lane_dot(a, b):
    return lax.dot_general(a, b, (((1,), (1,)), ((), ())), preferred_element_type=jnp.float32)


def hbm(value):
    return pltpu.with_memory_space_constraint(value, pltpu.HBM)


def share_rows(depth, number):
    eighth = depth // sum(SHARES)
    return sum(SHARES[:number]) * eighth, SHARES[number] * eighth


def share_copy(projection_hbm, buffer, sem, number):
    first, rows = share_rows(projection_hbm.shape[0], number)
    width = buffer.shape[1]
    columns = pl.ds(pl.multiple_of(lax.axis_index("ex") * width, 128), width)
    return pltpu.make_async_copy(projection_hbm.at[pl.ds(first, rows), columns], buffer, sem)


def share_shape(projection, number, ex_count):
    depth, width = projection.shape
    return share_rows(depth, number)[1], width // ex_count


def load_body(number, after_ref, projection_hbm, buffer, sem):
    copy = share_copy(projection_hbm, buffer, sem, number)
    copy.start()
    copy.wait()


def load(projection, number, ex_count, after):
    return pl.pallas_call(
        functools.partial(load_body, number),
        out_shape=pltpu.VMEM(share_shape(projection, number, ex_count), projection.dtype),
        in_specs=[VMEM, HBM],
        out_specs=VMEM,
        scratch_shapes=[pltpu.SemaphoreType.DMA],
        compiler_params=params(2),
    )(after, hbm(projection))


def gradient_body(chunks, counts, hidden_hbm, factor_hbm, cotangent_hbm, projection_hbm, lengths, order_hbm, *refs):
    ctx_count, feat_count, ex_count = counts
    outs, ranks_ref, share_ref = refs[:ctx_count], refs[ctx_count], refs[ctx_count + 1]
    hidden, factor, cotangent, blocks, order, sems, order_sem = refs[ctx_count + 2 :]
    own, tokens, width = hidden.shape
    part = width // chunks
    order_copy = pltpu.make_async_copy(order_hbm, order, order_sem)
    order_copy.start()
    copies = [pltpu.make_async_copy(factor_hbm, factor, sems.at[0])]
    for k in range(chunks):
        columns = pl.ds(k * part, part)
        copies.append(
            pltpu.make_async_copy(hidden_hbm.at[:, :, columns], hidden.at[:, :, columns], sems.at[1 + k])
        )
    copies.append(pltpu.make_async_copy(cotangent_hbm, cotangent, sems.at[1 + chunks]))
    copies.append(share_copy(projection_hbm, share_ref, sems.at[2 + chunks], 0))
    for copy in copies:
        copy.start()
    copies[0].wait()
    down = [None] * own
    for k in range(chunks):
        copies[1 + k].wait()
        for e in range(own):
            product = lane_dot(factor[:, k * part : (k + 1) * part], hidden[e, :, k * part : (k + 1) * part])
            down[e] = product if k == 0 else down[e] + product
    copies[-2].wait()
    order_copy.wait()
    place = lax.axis_index("ctx")
    for e in range(own):
        rows = down[e].astype(jnp.bfloat16)
        position = place * tokens + lax.broadcasted_iota(jnp.int32, rows.shape, 1)
        rows = jnp.where(position < lengths[e], rows.astype(jnp.float32), 0.0).astype(jnp.bfloat16)
        grad = jnp.dot(rows, cotangent[e], preferred_element_type=jnp.float32)
        share = grad.shape[0] // ctx_count
        for c in range(ctx_count):
            blocks[c, e] = grad[c * share : (c + 1) * share]
    for step in range(ctx_count):
        outs[step][...] = blocks[place_at(place, ctx_count, step)]
    feat, ex = lax.axis_index("feat"), lax.axis_index("ex")
    per_ex = own * feat_count
    for k, steps in enumerate(exchange_steps(feat_count, ex_count)):
        from_feat, from_ex = place_at(feat, feat_count, steps[0], -1), place_at(ex, ex_count, steps[1], -1)
        for e in range(own):
            wanted = order[(from_feat * ex_count + from_ex) * own + e]
            rank = step_to(ex, lax.div(wanted, per_ex), ex_count) * per_ex + lax.rem(wanted, per_ex)
            ranks_ref[pl.ds(k * own + e, 1), :] = jnp.full((1, 128), rank, jnp.int32)
    copies[-1].wait()


def gradient(hidden, factor, cotangent, projection, lengths, order, counts):
    ctx_count, feat_count, ex_count = counts
    own, tokens, width = hidden.shape
    rank, model = factor.shape[0], cotangent.shape[2]
    shape = (own, rank // ctx_count, model)
    chunks = 2
    return pl.pallas_call(
        functools.partial(gradient_body, chunks, counts),
        out_shape=[jax.ShapeDtypeStruct(shape, jnp.float32)] * ctx_count
        + [
            jax.ShapeDtypeStruct((own * feat_count * ex_count, 128), jnp.int32),
            pltpu.VMEM(share_shape(projection, 0, ex_count), projection.dtype),
        ],
        in_specs=[HBM] * 4 + [pl.BlockSpec(memory_space=pltpu.SMEM), HBM],
        out_specs=[VMEM] * (ctx_count + 2),
        scratch_shapes=[
            pltpu.VMEM(hidden.shape, hidden.dtype),
            pltpu.VMEM(factor.shape, factor.dtype),
            pltpu.VMEM(cotangent.shape, cotangent.dtype),
            pltpu.VMEM((ctx_count,) + shape, jnp.float32),
            pltpu.SMEM(order.shape, order.dtype),
            pltpu.SemaphoreType.DMA((chunks + 3,)),
            pltpu.SemaphoreType.DMA,
        ],
        compiler_params=params(8),
    )(*map(hbm, (hidden, factor, cotangent, projection)), lengths, hbm(order))


def sum_body(*refs):
    total = refs[0][...]
    for ref in refs[1:-2]:
        total = total + ref[...]
    refs[-1][...] = total.astype(refs[-1].dtype)


def sum_rows(parts, dtype, after):
    return pl.pallas_call(
        sum_body,
        out_shape=jax.ShapeDtypeStruct(parts[0].shape, dtype),
        in_specs=[VMEM] * (len(parts) + 1),
        out_specs=VMEM,
        compiler_params=params(2),
    )(*parts, pltpu.with_memory_space_constraint(after, pltpu.VMEM))


def project_body(source_count, ranks_ref, projection_hbm, *refs):
    sources, shares, (out, last_share, rows_ref, sem) = refs[:source_count], refs[source_count:-4], refs[-4:]
    copy = share_copy(projection_hbm, last_share, sem, len(shares))
    copy.start()
    padded, count = rows_ref.shape[0], out.shape[0]
    own, share, model = sources[0].shape
    row = lax.broadcasted_iota(jnp.int32, (padded, model), 0)
    ranks = ranks_ref[...][:, :1]
    for r in range(share):
        rows = jnp.zeros((padded, model), jnp.float32)
        for k, source in enumerate(sources):
            for e in range(own):
                values = source[e, r : r + 1].astype(jnp.float32)
                rows = rows + jnp.where(row == ranks[k * own + e : k * own + e + 1], values, 0.0)
        rows_ref[:, r * model : (r + 1) * model] = rows.astype(jnp.bfloat16)
    for number, weights in enumerate((*shares, last_share)):
        first, depth = share_rows(projection_hbm.shape[0], number)
        if number == len(shares):
            copy.wait()
        part = jnp.dot(rows_ref[:, first : first + depth], weights[...], preferred_element_type=jnp.float32)
        total = part if number == 0 else total + part
    out[...] = total[:count]


def project(sources, ranks, projection, shares, ex_count):
    depth, width = projection.shape
    count = ranks.shape[0]
    padded = max(8, count)
    return pl.pallas_call(
        functools.partial(project_body, len(sources)),
        out_shape=jax.ShapeDtypeStruct((count, width // ex_count), jnp.float32),
        in_specs=[VMEM, HBM] + [VMEM] * (len(sources) + len(shares)),
        out_specs=VMEM,
        scratch_shapes=[
            pltpu.VMEM(share_shape(projection, len(shares), ex_count), projection.dtype),
            pltpu.VMEM((padded, depth), jnp.bfloat16),
            pltpu.SemaphoreType.DMA,
        ],
        compiler_params=params(8),
    )(ranks, hbm(projection), *sources, *[pltpu.with_memory_space_constraint(v, pltpu.VMEM) for v in shares])


def total_body(ex_count, *refs):
    parts = refs[: -2 * ex_count - 1]
    near, *others, own_rows, own_squares = refs[-2 * ex_count - 1 :]
    total = parts[0][...]
    for part in parts[1:]:
        total = total + part[...]
    squares = jnp.sum(total * total, axis=1, keepdims=True)
    per_ex, width = own_rows.shape
    own_rows[...] = total[:per_ex]
    for step in range(ex_count):
        rows = slice(step * per_ex, (step + 1) * per_ex)
        spread = jnp.broadcast_to(squares[rows], (per_ex, 128))
        if step == 0:
            near[...] = spread
            own_squares[...] = spread
        else:
            others[2 * step - 2][:, :width] = total[rows]
            others[2 * step - 2][:, width:] = spread
            others[2 * step - 1][...] = spread


def totals(parts, ex_count):
    count, width = parts[0].shape
    per_ex = count // ex_count
    shape = lambda columns: jax.ShapeDtypeStruct((per_ex, columns), jnp.float32)
    near, *others, own_rows, own_squares = pl.pallas_call(
        functools.partial(total_body, ex_count),
        out_shape=[shape(128)] + [shape(width + 128), shape(128)] * (ex_count - 1) + [shape(width), shape(128)],
        in_specs=[VMEM] * len(parts),
        out_specs=[VMEM] * (2 * ex_count + 1),
        compiler_params=params(8),
    )(*parts)
    return [own_rows, *others[::2]], [near, *others[1::2]], own_squares


def scale_body(near_count, ex_count, columns, *refs):
    rows, squares, out = refs[near_count : near_count + ex_count], refs[:near_count] + refs[near_count + ex_count : -1], refs[-1]
    width = rows[0].shape[1]
    total = squares[0][...]
    for square in squares[1:]:
        total = total + square[...]
    for row in rows[1:]:
        total = total + row[:, width:]
    norm = jnp.sqrt(total[:, :1] / columns + 1e-06)
    for step in range(ex_count):
        place = place_at(lax.axis_index("ex"), ex_count, step, -1)
        out[:, pl.ds(pl.multiple_of(place * width, 128), width)] = rows[step][:, :width] / norm


def scale(near, rows, squares, columns):
    per_ex, width = rows[0].shape
    operands = (*near, *rows, *squares)
    return pl.pallas_call(
        functools.partial(scale_body, len(near), len(rows), columns),
        out_shape=jax.ShapeDtypeStruct((per_ex, width * len(rows)), jnp.float32),
        in_specs=[VMEM] * len(operands),
        out_specs=VMEM,
        compiler_params=params(8),
    )(*operands)


def per_device(hidden, cotangent, adapter_down_factor, projection, lengths, slot_example_order):
    counts = ctx_count, feat_count, ex_count = tuple(map(lax.axis_size, ("ctx", "feat", "ex")))
    ctx_steps = sorted(range(1, ctx_count), key=lambda s: (s == 1, s))
    chip_steps = exchange_steps(feat_count, ex_count)[1:]

    *blocks, ranks, share = gradient(
        hidden, adapter_down_factor.T, cotangent, projection, lengths, slot_example_order, counts
    )
    shares = [share, load(projection, 1, ex_count, ranks)]
    grad_rows = sum_rows(
        [blocks[0]] + [swap(blocks[s], ("ctx",), (s,)) for s in reversed(ctx_steps)], jnp.bfloat16, shares[1]
    )
    shares.append(load(projection, 2, ex_count, grad_rows))
    sources = [grad_rows] + [swap(grad_rows, ("feat", "ex"), s) for s in chip_steps]
    product = project(sources, ranks, projection, shares, ex_count)
    rows, squares, own_squares = totals([product] + [swap(product, ("ctx",), (s,)) for s in reversed(ctx_steps)], ex_count)
    taken = [rows[0]] + [swap(rows[s], ("ex",), (s,)) for s in range(1, ex_count)]
    near, far = (
        [swap(squares[e], ("feat", "ex"), (f, e)) for f, e in chip_steps if f and bool(e) == both] for both in (False, True)
    )
    return scale(near, taken, [*far, own_squares], projection.shape[1] * feat_count)


def solution(mesh):
    in_specs = (
        P(("group", "feat", "ex"), "ctx", None),
        P(("group", "feat", "ex"), "ctx", None),
        P(),
        P("ctx", "feat"),
        P(("group", "feat", "ex")),
        P("group"),
    )
    out_specs = P(("group", "ex"), "feat")
    return jax.shard_map(
        per_device, mesh=mesh, in_specs=in_specs, out_specs=out_specs, check_vma=False
    )
```

```python
import functools
import itertools

import jax
import jax.numpy as jnp
from jax import lax
from jax.experimental import pallas as pl
from jax.experimental.pallas import tpu as pltpu
from jax.sharding import PartitionSpec as P

MIB = 1 << 20
VMEM = pl.BlockSpec(memory_space=pltpu.VMEM)
HBM = pl.BlockSpec(memory_space=pltpu.HBM)


def is_power(count):
    return count & (count - 1) == 0


def place_at(index, count, step, sign=1):
    if is_power(count):
        return index ^ step
    return (index + sign * step + count) % count


def step_to(index, target, count):
    if is_power(count):
        return index ^ target
    return lax.rem(target - index + count, count)


def exchange_steps(feat_count, ex_count):
    steps = itertools.product(range(feat_count), range(ex_count))
    return sorted(steps, key=lambda s: (any(s), not all(s), s))


def swap(value, axes, steps):
    sizes = [lax.axis_size(a) for a in axes]
    flat = lambda place: functools.reduce(lambda total, p: total * p[1] + p[0], zip(place, sizes), 0)
    pairs = [
        (flat(place), flat([place_at(i, n, s) for i, n, s in zip(place, sizes, steps)]))
        for place in itertools.product(*map(range, sizes))
    ]
    return lax.ppermute(value, tuple(axes) if len(axes) > 1 else axes[0], pairs)


def params(mib, **more):
    return pltpu.CompilerParams(vmem_limit_bytes=int(mib * MIB), **more)


def lane_dot(a, b):
    return lax.dot_general(a, b, (((1,), (1,)), ((), ())), preferred_element_type=jnp.float32)


def hbm(value):
    return pltpu.with_memory_space_constraint(value, pltpu.HBM)


def gradient_body(chunks, ctx_count, hidden_hbm, factor_hbm, cotangent_hbm, lengths, *refs):
    outs, (hidden, factor, cotangent, blocks, sems) = refs[:ctx_count], refs[ctx_count:]
    own, tokens, width = hidden.shape
    part = width // chunks
    copies = [pltpu.make_async_copy(factor_hbm, factor, sems.at[0])]
    for k in range(chunks):
        columns = pl.ds(k * part, part)
        copies.append(
            pltpu.make_async_copy(hidden_hbm.at[:, :, columns], hidden.at[:, :, columns], sems.at[1 + k])
        )
    copies.append(pltpu.make_async_copy(cotangent_hbm, cotangent, sems.at[1 + chunks]))
    for copy in copies:
        copy.start()
    copies[0].wait()
    down = [None] * own
    for k in range(chunks):
        copies[1 + k].wait()
        for e in range(own):
            product = lane_dot(factor[:, k * part : (k + 1) * part], hidden[e, :, k * part : (k + 1) * part])
            down[e] = product if k == 0 else down[e] + product
    copies[-1].wait()
    place = lax.axis_index("ctx")
    for e in range(own):
        rows = down[e].astype(jnp.bfloat16)
        position = place * tokens + lax.broadcasted_iota(jnp.int32, rows.shape, 1)
        rows = jnp.where(position < lengths[e], rows.astype(jnp.float32), 0.0).astype(jnp.bfloat16)
        grad = jnp.dot(rows, cotangent[e], preferred_element_type=jnp.float32)
        share = grad.shape[0] // ctx_count
        for c in range(ctx_count):
            blocks[c, e] = grad[c * share : (c + 1) * share]
    for step in range(ctx_count):
        outs[step][...] = blocks[place_at(place, ctx_count, step)]


def gradient(hidden, factor, cotangent, lengths, ctx_count):
    own, tokens, width = hidden.shape
    rank, model = factor.shape[0], cotangent.shape[2]
    shape = (own, rank // ctx_count, model)
    chunks = 2
    return pl.pallas_call(
        functools.partial(gradient_body, chunks, ctx_count),
        out_shape=[jax.ShapeDtypeStruct(shape, jnp.float32)] * ctx_count,
        in_specs=[HBM] * 3 + [pl.BlockSpec(memory_space=pltpu.SMEM)],
        out_specs=[VMEM] * ctx_count,
        scratch_shapes=[
            pltpu.VMEM(hidden.shape, hidden.dtype),
            pltpu.VMEM(factor.shape, factor.dtype),
            pltpu.VMEM(cotangent.shape, cotangent.dtype),
            pltpu.VMEM((ctx_count,) + shape, jnp.float32),
            pltpu.SemaphoreType.DMA((chunks + 2,)),
        ],
        compiler_params=params(4),
    )(*map(hbm, (hidden, factor, cotangent)), lengths)


def sum_body(*refs):
    total = refs[0][...]
    for ref in refs[1:-1]:
        total = total + ref[...]
    refs[-1][...] = total.astype(refs[-1].dtype)


def sum_rows(parts, dtype):
    return pl.pallas_call(
        sum_body,
        out_shape=jax.ShapeDtypeStruct(parts[0].shape, dtype),
        in_specs=[VMEM] * len(parts),
        out_specs=VMEM,
        compiler_params=params(2),
    )(*parts)


def project_body(feat_count, ex_count, order_ref, held_ref, *refs):
    sources, (out, rows_ref) = refs[:-2], refs[-2:]
    count, width = out.shape
    own, share, model = sources[0].shape
    feat, ex = lax.axis_index("feat"), lax.axis_index("ex")
    per_ex = own * feat_count
    order = order_ref[...]
    slot = lax.broadcasted_iota(jnp.int32, order.shape, 1)
    ranks = []
    for steps in exchange_steps(feat_count, ex_count):
        from_feat, from_ex = place_at(feat, feat_count, steps[0], -1), place_at(ex, ex_count, steps[1], -1)
        for e in range(own):
            chosen = slot == (from_feat * ex_count + from_ex) * own + e
            wanted = jnp.sum(jnp.where(chosen, order, 0), axis=1, keepdims=True)
            target = sum((wanted >= j * per_ex).astype(jnp.int32) for j in range(1, ex_count))
            ranks.append(step_to(ex, target, ex_count) * per_ex + wanted - target * per_ex)
    row = lax.broadcasted_iota(jnp.int32, (rows_ref.shape[0], model), 0)
    for r in range(share):
        rows = jnp.zeros(row.shape, jnp.float32)
        for k, source in enumerate(sources):
            for e in range(own):
                values = source[e, r : r + 1].astype(jnp.float32)
                rows = rows + jnp.where(row == ranks[k * own + e], values, 0.0)
        rows_ref[:, r * model : (r + 1) * model] = rows.astype(jnp.bfloat16)
    columns = pl.ds(pl.multiple_of(ex * width, 128), width)
    out[...] = jnp.dot(rows_ref[...], held_ref[:, columns], preferred_element_type=jnp.float32)[:count]


def project(sources, order, held, feat_count, ex_count):
    depth, width = held.shape
    count = len(sources) * sources[0].shape[0]
    padded = max(8, count)
    return pl.pallas_call(
        functools.partial(project_body, feat_count, ex_count),
        out_shape=jax.ShapeDtypeStruct((count, width // ex_count), jnp.float32),
        in_specs=[VMEM] * (len(sources) + 2),
        out_specs=VMEM,
        scratch_shapes=[pltpu.VMEM((padded, depth), jnp.bfloat16)],
        compiler_params=params(2 + 60 / 1024),
    )(order.reshape(1, -1), pltpu.with_memory_space_constraint(held, pltpu.VMEM), *sources)


def total_body(ex_count, *refs):
    parts = refs[: -2 * ex_count - 1]
    near, *others, own_rows, own_squares = refs[-2 * ex_count - 1 :]
    total = parts[0][...]
    for part in parts[1:]:
        total = total + part[...]
    squares = jnp.sum(total * total, axis=1, keepdims=True)
    per_ex, width = own_rows.shape
    own_rows[...] = total[:per_ex]
    for step in range(ex_count):
        rows = slice(step * per_ex, (step + 1) * per_ex)
        spread = jnp.broadcast_to(squares[rows], (per_ex, 128))
        if step == 0:
            near[...] = spread
            own_squares[...] = spread
        else:
            others[2 * step - 2][:, :width] = total[rows]
            others[2 * step - 2][:, width:] = spread
            others[2 * step - 1][...] = spread


def totals(parts, ex_count):
    count, width = parts[0].shape
    per_ex = count // ex_count
    shape = lambda columns: jax.ShapeDtypeStruct((per_ex, columns), jnp.float32)
    near, *others, own_rows, own_squares = pl.pallas_call(
        functools.partial(total_body, ex_count),
        out_shape=[shape(128)] + [shape(width + 128), shape(128)] * (ex_count - 1) + [shape(width), shape(128)],
        in_specs=[VMEM] * len(parts),
        out_specs=[VMEM] * (2 * ex_count + 1),
        compiler_params=params(1),
    )(*parts)
    return [own_rows, *others[::2]], [near, *others[1::2]], own_squares


def scale_body(near_count, ex_count, columns, *refs):
    rows, squares, out = refs[near_count : near_count + ex_count], refs[:near_count] + refs[near_count + ex_count : -1], refs[-1]
    width = rows[0].shape[1]
    total = squares[0][...]
    for square in squares[1:]:
        total = total + square[...]
    for row in rows[1:]:
        total = total + row[:, width:]
    norm = jnp.sqrt(total[:, :1] / columns + 1e-06)
    for step in range(ex_count):
        place = place_at(lax.axis_index("ex"), ex_count, step, -1)
        out[:, pl.ds(pl.multiple_of(place * width, 128), width)] = rows[step][:, :width] / norm


def scale(near, rows, squares, columns):
    per_ex, width = rows[0].shape
    operands = (*near, *rows, *squares)
    return pl.pallas_call(
        functools.partial(scale_body, len(near), len(rows), columns),
        out_shape=jax.ShapeDtypeStruct((per_ex, width * len(rows)), jnp.float32),
        in_specs=[VMEM] * len(operands),
        out_specs=VMEM,
        compiler_params=params(1),
    )(*operands)


def per_device(hidden, cotangent, adapter_down_factor, projection, lengths, slot_example_order):
    ctx_count, feat_count, ex_count = tuple(map(lax.axis_size, ("ctx", "feat", "ex")))
    ctx_steps = sorted(range(1, ctx_count), key=lambda s: (s == 1, s))
    chip_steps = exchange_steps(feat_count, ex_count)[1:]

    blocks = gradient(hidden, adapter_down_factor.T, cotangent, lengths, ctx_count)
    later, first = lax.optimization_barrier((projection, blocks[0]))
    held = lax.ppermute(later, "ex", [(i, i) for i in range(ex_count)])
    grad_rows = sum_rows([first] + [swap(blocks[s], ("ctx",), (s,)) for s in ctx_steps], jnp.bfloat16)
    sources = [grad_rows] + [swap(grad_rows, ("feat", "ex"), s) for s in chip_steps]
    product = project(sources, slot_example_order, held, feat_count, ex_count)
    rows, squares, own_squares = totals([product] + [swap(product, ("ctx",), (s,)) for s in reversed(ctx_steps)], ex_count)
    taken = [rows[0]] + [swap(rows[s], ("ex",), (s,)) for s in range(1, ex_count)]
    near, far = (
        [swap(squares[e], ("feat", "ex"), (f, e)) for f, e in chip_steps if f and bool(e) == both] for both in (False, True)
    )
    return scale(near, taken, [*far, own_squares], projection.shape[1] * feat_count)


def solution(mesh):
    in_specs = (
        P(("group", "feat", "ex"), "ctx", None),
        P(("group", "feat", "ex"), "ctx", None),
        P(),
        P("ctx", "feat"),
        P(("group", "feat", "ex")),
        P("group"),
    )
    out_specs = P(("group", "ex"), "feat")
    return jax.shard_map(
        per_device, mesh=mesh, in_specs=in_specs, out_specs=out_specs, check_vma=False
    )
```

```python
import functools
import itertools

import jax
import jax.numpy as jnp
from jax import lax
from jax.experimental import pallas as pl
from jax.experimental.pallas import tpu as pltpu
from jax.sharding import PartitionSpec as P

MIB = 1 << 20
SHARES = (1, 4, 3)
VMEM = pl.BlockSpec(memory_space=pltpu.VMEM)
HBM = pl.BlockSpec(memory_space=pltpu.HBM)


def is_power(count):
    return count & (count - 1) == 0


def place_at(index, count, step, sign=1):
    if is_power(count):
        return index ^ step
    return (index + sign * step + count) % count


def step_to(index, target, count):
    if is_power(count):
        return index ^ target
    return lax.rem(target - index + count, count)


def exchange_steps(feat_count, ex_count):
    steps = itertools.product(range(feat_count), range(ex_count))
    return sorted(steps, key=lambda s: (any(s), not all(s), s))


def swap(value, axes, steps):
    sizes = [lax.axis_size(a) for a in axes]
    flat = lambda place: functools.reduce(lambda total, p: total * p[1] + p[0], zip(place, sizes), 0)
    pairs = [
        (flat(place), flat([place_at(i, n, s) for i, n, s in zip(place, sizes, steps)]))
        for place in itertools.product(*map(range, sizes))
    ]
    return lax.ppermute(value, tuple(axes) if len(axes) > 1 else axes[0], pairs)


def params(mib, **more):
    return pltpu.CompilerParams(vmem_limit_bytes=mib * MIB, **more)


def lane_dot(a, b):
    return lax.dot_general(a, b, (((1,), (1,)), ((), ())), preferred_element_type=jnp.float32)


def hbm(value):
    return pltpu.with_memory_space_constraint(value, pltpu.HBM)


def share_rows(depth, number):
    eighth = depth // sum(SHARES)
    return sum(SHARES[:number]) * eighth, SHARES[number] * eighth


def share_copy(projection_hbm, buffer, sem, number):
    first, rows = share_rows(projection_hbm.shape[0], number)
    width = buffer.shape[1]
    columns = pl.ds(pl.multiple_of(lax.axis_index("ex") * width, 128), width)
    return pltpu.make_async_copy(projection_hbm.at[pl.ds(first, rows), columns], buffer, sem)


def share_shape(projection, number, ex_count):
    depth, width = projection.shape
    return share_rows(depth, number)[1], width // ex_count


def load_body(number, after_ref, projection_hbm, buffer, sem):
    copy = share_copy(projection_hbm, buffer, sem, number)
    copy.start()
    copy.wait()


def load(projection, number, ex_count, after):
    return pl.pallas_call(
        functools.partial(load_body, number),
        out_shape=pltpu.VMEM(share_shape(projection, number, ex_count), projection.dtype),
        in_specs=[VMEM, HBM],
        out_specs=VMEM,
        scratch_shapes=[pltpu.SemaphoreType.DMA],
        compiler_params=params(2),
    )(after, hbm(projection))


def gradient_body(chunks, counts, hidden_hbm, factor_hbm, cotangent_hbm, projection_hbm, lengths, order_hbm, *refs):
    ctx_count, feat_count, ex_count = counts
    outs, ranks_ref, share_ref = refs[:ctx_count], refs[ctx_count], refs[ctx_count + 1]
    hidden, factor, cotangent, blocks, order, sems, order_sem = refs[ctx_count + 2 :]
    own, tokens, width = hidden.shape
    part = width // chunks
    order_copy = pltpu.make_async_copy(order_hbm, order, order_sem)
    order_copy.start()
    copies = [pltpu.make_async_copy(factor_hbm, factor, sems.at[0])]
    for k in range(chunks):
        columns = pl.ds(k * part, part)
        copies.append(
            pltpu.make_async_copy(hidden_hbm.at[:, :, columns], hidden.at[:, :, columns], sems.at[1 + k])
        )
    copies.append(pltpu.make_async_copy(cotangent_hbm, cotangent, sems.at[1 + chunks]))
    copies.append(share_copy(projection_hbm, share_ref, sems.at[2 + chunks], 0))
    for copy in copies:
        copy.start()
    copies[0].wait()
    down = [None] * own
    for k in range(chunks):
        copies[1 + k].wait()
        for e in range(own):
            product = lane_dot(factor[:, k * part : (k + 1) * part], hidden[e, :, k * part : (k + 1) * part])
            down[e] = product if k == 0 else down[e] + product
    copies[-2].wait()
    order_copy.wait()
    place = lax.axis_index("ctx")
    for e in range(own):
        rows = down[e].astype(jnp.bfloat16)
        position = place * tokens + lax.broadcasted_iota(jnp.int32, rows.shape, 1)
        rows = jnp.where(position < lengths[e], rows.astype(jnp.float32), 0.0).astype(jnp.bfloat16)
        grad = jnp.dot(rows, cotangent[e], preferred_element_type=jnp.float32)
        share = grad.shape[0] // ctx_count
        for c in range(ctx_count):
            blocks[c, e] = grad[c * share : (c + 1) * share]
    for step in range(ctx_count):
        outs[step][...] = blocks[place_at(place, ctx_count, step)]
    feat, ex = lax.axis_index("feat"), lax.axis_index("ex")
    per_ex = own * feat_count
    for k, steps in enumerate(exchange_steps(feat_count, ex_count)):
        from_feat, from_ex = place_at(feat, feat_count, steps[0], -1), place_at(ex, ex_count, steps[1], -1)
        for e in range(own):
            wanted = order[(from_feat * ex_count + from_ex) * own + e]
            rank = step_to(ex, lax.div(wanted, per_ex), ex_count) * per_ex + lax.rem(wanted, per_ex)
            ranks_ref[pl.ds(k * own + e, 1), :] = jnp.full((1, 128), rank, jnp.int32)
    copies[-1].wait()


def gradient(hidden, factor, cotangent, projection, lengths, order, counts):
    ctx_count, feat_count, ex_count = counts
    own, tokens, width = hidden.shape
    rank, model = factor.shape[0], cotangent.shape[2]
    shape = (own, rank // ctx_count, model)
    chunks = 2
    return pl.pallas_call(
        functools.partial(gradient_body, chunks, counts),
        out_shape=[jax.ShapeDtypeStruct(shape, jnp.float32)] * ctx_count
        + [
            jax.ShapeDtypeStruct((own * feat_count * ex_count, 128), jnp.int32),
            pltpu.VMEM(share_shape(projection, 0, ex_count), projection.dtype),
        ],
        in_specs=[HBM] * 4 + [pl.BlockSpec(memory_space=pltpu.SMEM), HBM],
        out_specs=[VMEM] * (ctx_count + 2),
        scratch_shapes=[
            pltpu.VMEM(hidden.shape, hidden.dtype),
            pltpu.VMEM(factor.shape, factor.dtype),
            pltpu.VMEM(cotangent.shape, cotangent.dtype),
            pltpu.VMEM((ctx_count,) + shape, jnp.float32),
            pltpu.SMEM(order.shape, order.dtype),
            pltpu.SemaphoreType.DMA((chunks + 3,)),
            pltpu.SemaphoreType.DMA,
        ],
        compiler_params=params(8),
    )(*map(hbm, (hidden, factor, cotangent, projection)), lengths, hbm(order))


def sum_body(*refs):
    total = refs[0][...]
    for ref in refs[1:-2]:
        total = total + ref[...]
    refs[-1][...] = total.astype(refs[-1].dtype)


def sum_rows(parts, dtype, after):
    return pl.pallas_call(
        sum_body,
        out_shape=jax.ShapeDtypeStruct(parts[0].shape, dtype),
        in_specs=[VMEM] * (len(parts) + 1),
        out_specs=VMEM,
        compiler_params=params(2),
    )(*parts, pltpu.with_memory_space_constraint(after, pltpu.VMEM))


def project_body(source_count, ranks_ref, *refs):
    sources, shares, (out, rows_ref) = refs[:source_count], refs[source_count:-2], refs[-2:]
    padded, count = rows_ref.shape[0], out.shape[0]
    own, share, model = sources[0].shape
    row = lax.broadcasted_iota(jnp.int32, (padded, model), 0)
    ranks = ranks_ref[...][:, :1]
    for r in range(share):
        rows = jnp.zeros((padded, model), jnp.float32)
        for k, source in enumerate(sources):
            for e in range(own):
                values = source[e, r : r + 1].astype(jnp.float32)
                rows = rows + jnp.where(row == ranks[k * own + e : k * own + e + 1], values, 0.0)
        rows_ref[:, r * model : (r + 1) * model] = rows.astype(jnp.bfloat16)
    for number, weights in enumerate(shares):
        first, depth = share_rows(rows_ref.shape[1], number)
        part = jnp.dot(rows_ref[:, first : first + depth], weights[...], preferred_element_type=jnp.float32)
        total = part if number == 0 else total + part
    out[...] = total[:count]


def project(sources, ranks, projection, shares, ex_count):
    depth, width = projection.shape
    count = ranks.shape[0]
    padded = max(8, count)
    return pl.pallas_call(
        functools.partial(project_body, len(sources)),
        out_shape=jax.ShapeDtypeStruct((count, width // ex_count), jnp.float32),
        in_specs=[VMEM] * (1 + len(sources) + len(shares)),
        out_specs=VMEM,
        scratch_shapes=[
            pltpu.VMEM((padded, depth), jnp.bfloat16),
        ],
        compiler_params=params(8),
    )(ranks, *sources, *[pltpu.with_memory_space_constraint(v, pltpu.VMEM) for v in shares])


def total_body(ex_count, *refs):
    parts = refs[: -2 * ex_count - 1]
    near, *others, own_rows, own_squares = refs[-2 * ex_count - 1 :]
    total = parts[0][...]
    for part in parts[1:]:
        total = total + part[...]
    squares = jnp.sum(total * total, axis=1, keepdims=True)
    per_ex, width = own_rows.shape
    own_rows[...] = total[:per_ex]
    for step in range(ex_count):
        rows = slice(step * per_ex, (step + 1) * per_ex)
        spread = jnp.broadcast_to(squares[rows], (per_ex, 128))
        if step == 0:
            near[...] = spread
            own_squares[...] = spread
        else:
            others[2 * step - 2][:, :width] = total[rows]
            others[2 * step - 2][:, width:] = spread
            others[2 * step - 1][...] = spread


def totals(parts, ex_count):
    count, width = parts[0].shape
    per_ex = count // ex_count
    shape = lambda columns: jax.ShapeDtypeStruct((per_ex, columns), jnp.float32)
    near, *others, own_rows, own_squares = pl.pallas_call(
        functools.partial(total_body, ex_count),
        out_shape=[shape(128)] + [shape(width + 128), shape(128)] * (ex_count - 1) + [shape(width), shape(128)],
        in_specs=[VMEM] * len(parts),
        out_specs=[VMEM] * (2 * ex_count + 1),
        compiler_params=params(8),
    )(*parts)
    return [own_rows, *others[::2]], [near, *others[1::2]], own_squares


def scale_body(near_count, ex_count, columns, *refs):
    rows, squares, out = refs[near_count : near_count + ex_count], refs[:near_count] + refs[near_count + ex_count : -1], refs[-1]
    width = rows[0].shape[1]
    total = squares[0][...]
    for square in squares[1:]:
        total = total + square[...]
    for row in rows[1:]:
        total = total + row[:, width:]
    norm = jnp.sqrt(total[:, :1] / columns + 1e-06)
    for step in range(ex_count):
        place = place_at(lax.axis_index("ex"), ex_count, step, -1)
        out[:, pl.ds(pl.multiple_of(place * width, 128), width)] = rows[step][:, :width] / norm


def scale(near, rows, squares, columns):
    per_ex, width = rows[0].shape
    operands = (*near, *rows, *squares)
    return pl.pallas_call(
        functools.partial(scale_body, len(near), len(rows), columns),
        out_shape=jax.ShapeDtypeStruct((per_ex, width * len(rows)), jnp.float32),
        in_specs=[VMEM] * len(operands),
        out_specs=VMEM,
        compiler_params=params(8),
    )(*operands)


def per_device(hidden, cotangent, adapter_down_factor, projection, lengths, slot_example_order):
    counts = ctx_count, feat_count, ex_count = tuple(map(lax.axis_size, ("ctx", "feat", "ex")))
    ctx_steps = sorted(range(1, ctx_count), key=lambda s: (s == 1, s))
    chip_steps = exchange_steps(feat_count, ex_count)[1:]

    *blocks, ranks, share = gradient(
        hidden, adapter_down_factor.T, cotangent, projection, lengths, slot_example_order, counts
    )
    shares = [share, load(projection, 1, ex_count, ranks)]
    grad_rows = sum_rows(
        [blocks[0]] + [swap(blocks[s], ("ctx",), (s,)) for s in ctx_steps], jnp.bfloat16, shares[1]
    )
    shares.append(load(projection, 2, ex_count, grad_rows))
    sources = [grad_rows] + [swap(grad_rows, ("feat", "ex"), s) for s in chip_steps]
    product = project(sources, ranks, projection, shares, ex_count)
    rows, squares, own_squares = totals([product] + [swap(product, ("ctx",), (s,)) for s in reversed(ctx_steps)], ex_count)
    taken = [rows[0]] + [swap(rows[s], ("ex",), (s,)) for s in range(1, ex_count)]
    near, far = (
        [swap(squares[e], ("feat", "ex"), (f, e)) for f, e in chip_steps if f and bool(e) == both] for both in (False, True)
    )
    return scale(near, taken, [*far, own_squares], projection.shape[1] * feat_count)


def solution(mesh):
    in_specs = (
        P(("group", "feat", "ex"), "ctx", None),
        P(("group", "feat", "ex"), "ctx", None),
        P(),
        P("ctx", "feat"),
        P(("group", "feat", "ex")),
        P("group"),
    )
    out_specs = P(("group", "ex"), "feat")
    return jax.shard_map(
        per_device, mesh=mesh, in_specs=in_specs, out_specs=out_specs, check_vma=False
    )
```

```python
import functools
import itertools

import jax
import jax.numpy as jnp
from jax import lax
from jax.experimental import pallas as pl
from jax.experimental.pallas import tpu as pltpu
from jax.sharding import PartitionSpec as P

MIB = 1 << 20
SHARES = (2, 3, 3)
VMEM = pl.BlockSpec(memory_space=pltpu.VMEM)
HBM = pl.BlockSpec(memory_space=pltpu.HBM)


def is_power(count):
    return count & (count - 1) == 0


def place_at(index, count, step, sign=1):
    if is_power(count):
        return index ^ step
    return (index + sign * step + count) % count


def step_to(index, target, count):
    if is_power(count):
        return index ^ target
    return lax.rem(target - index + count, count)


def exchange_steps(feat_count, ex_count):
    steps = itertools.product(range(feat_count), range(ex_count))
    return sorted(steps, key=lambda s: (any(s), not all(s), s))


def swap(value, axes, steps):
    sizes = [lax.axis_size(a) for a in axes]
    flat = lambda place: functools.reduce(lambda total, p: total * p[1] + p[0], zip(place, sizes), 0)
    pairs = [
        (flat(place), flat([place_at(i, n, s) for i, n, s in zip(place, sizes, steps)]))
        for place in itertools.product(*map(range, sizes))
    ]
    return lax.ppermute(value, tuple(axes) if len(axes) > 1 else axes[0], pairs)


def params(mib, **more):
    return pltpu.CompilerParams(vmem_limit_bytes=mib * MIB, **more)


def lane_dot(a, b):
    return lax.dot_general(a, b, (((1,), (1,)), ((), ())), preferred_element_type=jnp.float32)


def hbm(value):
    return pltpu.with_memory_space_constraint(value, pltpu.HBM)


def share_rows(depth, number):
    eighth = depth // sum(SHARES)
    return sum(SHARES[:number]) * eighth, SHARES[number] * eighth


def share_copy(projection_hbm, buffer, sem, number):
    first, rows = share_rows(projection_hbm.shape[0], number)
    width = buffer.shape[1]
    columns = pl.ds(pl.multiple_of(lax.axis_index("ex") * width, 128), width)
    return pltpu.make_async_copy(projection_hbm.at[pl.ds(first, rows), columns], buffer, sem)


def share_shape(projection, number, ex_count):
    depth, width = projection.shape
    return share_rows(depth, number)[1], width // ex_count


def load_body(number, after_ref, projection_hbm, buffer, sem):
    copy = share_copy(projection_hbm, buffer, sem, number)
    copy.start()
    copy.wait()


def load(projection, number, ex_count, after):
    return pl.pallas_call(
        functools.partial(load_body, number),
        out_shape=pltpu.VMEM(share_shape(projection, number, ex_count), projection.dtype),
        in_specs=[VMEM, HBM],
        out_specs=VMEM,
        scratch_shapes=[pltpu.SemaphoreType.DMA],
        compiler_params=params(2),
    )(after, hbm(projection))


def gradient_body(chunks, counts, hidden_hbm, factor_hbm, cotangent_hbm, projection_hbm, lengths, order_hbm, *refs):
    ctx_count, feat_count, ex_count = counts
    outs, ranks_ref, share_ref = refs[:ctx_count], refs[ctx_count], refs[ctx_count + 1]
    hidden, factor, cotangent, blocks, order, sems, order_sem = refs[ctx_count + 2 :]
    own, tokens, width = hidden.shape
    part = width // chunks
    order_copy = pltpu.make_async_copy(order_hbm, order, order_sem)
    order_copy.start()
    copies = [pltpu.make_async_copy(factor_hbm, factor, sems.at[0])]
    for k in range(chunks):
        columns = pl.ds(k * part, part)
        copies.append(
            pltpu.make_async_copy(hidden_hbm.at[:, :, columns], hidden.at[:, :, columns], sems.at[1 + k])
        )
    copies.append(pltpu.make_async_copy(cotangent_hbm, cotangent, sems.at[1 + chunks]))
    copies.append(share_copy(projection_hbm, share_ref, sems.at[2 + chunks], 0))
    for copy in copies:
        copy.start()
    copies[0].wait()
    down = [None] * own
    for k in range(chunks):
        copies[1 + k].wait()
        for e in range(own):
            product = lane_dot(factor[:, k * part : (k + 1) * part], hidden[e, :, k * part : (k + 1) * part])
            down[e] = product if k == 0 else down[e] + product
    copies[-2].wait()
    order_copy.wait()
    place = lax.axis_index("ctx")
    for e in range(own):
        rows = down[e].astype(jnp.bfloat16)
        position = place * tokens + lax.broadcasted_iota(jnp.int32, rows.shape, 1)
        rows = jnp.where(position < lengths[e], rows.astype(jnp.float32), 0.0).astype(jnp.bfloat16)
        grad = jnp.dot(rows, cotangent[e], preferred_element_type=jnp.float32)
        share = grad.shape[0] // ctx_count
        for c in range(ctx_count):
            blocks[c, e] = grad[c * share : (c + 1) * share]
    for step in range(ctx_count):
        outs[step][...] = blocks[place_at(place, ctx_count, step)]
    feat, ex = lax.axis_index("feat"), lax.axis_index("ex")
    per_ex = own * feat_count
    for k, steps in enumerate(exchange_steps(feat_count, ex_count)):
        from_feat, from_ex = place_at(feat, feat_count, steps[0], -1), place_at(ex, ex_count, steps[1], -1)
        for e in range(own):
            wanted = order[(from_feat * ex_count + from_ex) * own + e]
            rank = step_to(ex, lax.div(wanted, per_ex), ex_count) * per_ex + lax.rem(wanted, per_ex)
            ranks_ref[pl.ds(k * own + e, 1), :] = jnp.full((1, 128), rank, jnp.int32)
    copies[-1].wait()


def gradient(hidden, factor, cotangent, projection, lengths, order, counts):
    ctx_count, feat_count, ex_count = counts
    own, tokens, width = hidden.shape
    rank, model = factor.shape[0], cotangent.shape[2]
    shape = (own, rank // ctx_count, model)
    chunks = 2
    return pl.pallas_call(
        functools.partial(gradient_body, chunks, counts),
        out_shape=[jax.ShapeDtypeStruct(shape, jnp.float32)] * ctx_count
        + [
            jax.ShapeDtypeStruct((own * feat_count * ex_count, 128), jnp.int32),
            pltpu.VMEM(share_shape(projection, 0, ex_count), projection.dtype),
        ],
        in_specs=[HBM] * 4 + [pl.BlockSpec(memory_space=pltpu.SMEM), HBM],
        out_specs=[VMEM] * (ctx_count + 2),
        scratch_shapes=[
            pltpu.VMEM(hidden.shape, hidden.dtype),
            pltpu.VMEM(factor.shape, factor.dtype),
            pltpu.VMEM(cotangent.shape, cotangent.dtype),
            pltpu.VMEM((ctx_count,) + shape, jnp.float32),
            pltpu.SMEM(order.shape, order.dtype),
            pltpu.SemaphoreType.DMA((chunks + 3,)),
            pltpu.SemaphoreType.DMA,
        ],
        compiler_params=params(8),
    )(*map(hbm, (hidden, factor, cotangent, projection)), lengths, hbm(order))


def sum_body(*refs):
    total = refs[0][...]
    for ref in refs[1:-2]:
        total = total + ref[...]
    refs[-1][...] = total.astype(refs[-1].dtype)


def sum_rows(parts, dtype, after):
    return pl.pallas_call(
        sum_body,
        out_shape=jax.ShapeDtypeStruct(parts[0].shape, dtype),
        in_specs=[VMEM] * (len(parts) + 1),
        out_specs=VMEM,
        compiler_params=params(2),
    )(*parts, pltpu.with_memory_space_constraint(after, pltpu.VMEM))


def project_body(source_count, ranks_ref, *refs):
    sources, shares, (out, rows_ref) = refs[:source_count], refs[source_count:-2], refs[-2:]
    padded, count = rows_ref.shape[0], out.shape[0]
    own, share, model = sources[0].shape
    row = lax.broadcasted_iota(jnp.int32, (padded, model), 0)
    ranks = ranks_ref[...][:, :1]
    for r in range(share):
        rows = jnp.zeros((padded, model), jnp.float32)
        for k, source in enumerate(sources):
            for e in range(own):
                values = source[e, r : r + 1].astype(jnp.float32)
                rows = rows + jnp.where(row == ranks[k * own + e : k * own + e + 1], values, 0.0)
        rows_ref[:, r * model : (r + 1) * model] = rows.astype(jnp.bfloat16)
    for number, weights in enumerate(shares):
        first, depth = share_rows(rows_ref.shape[1], number)
        part = jnp.dot(rows_ref[:, first : first + depth], weights[...], preferred_element_type=jnp.float32)
        total = part if number == 0 else total + part
    out[...] = total[:count]


def project(sources, ranks, projection, shares, ex_count):
    depth, width = projection.shape
    count = ranks.shape[0]
    padded = max(8, count)
    return pl.pallas_call(
        functools.partial(project_body, len(sources)),
        out_shape=jax.ShapeDtypeStruct((count, width // ex_count), jnp.float32),
        in_specs=[VMEM] * (1 + len(sources) + len(shares)),
        out_specs=VMEM,
        scratch_shapes=[
            pltpu.VMEM((padded, depth), jnp.bfloat16),
        ],
        compiler_params=params(8),
    )(ranks, *sources, *[pltpu.with_memory_space_constraint(v, pltpu.VMEM) for v in shares])


def total_body(ex_count, *refs):
    parts = refs[: -2 * ex_count - 1]
    near, *others, own_rows, own_squares = refs[-2 * ex_count - 1 :]
    total = parts[0][...]
    for part in parts[1:]:
        total = total + part[...]
    squares = jnp.sum(total * total, axis=1, keepdims=True)
    per_ex, width = own_rows.shape
    own_rows[...] = total[:per_ex]
    for step in range(ex_count):
        rows = slice(step * per_ex, (step + 1) * per_ex)
        spread = jnp.broadcast_to(squares[rows], (per_ex, 128))
        if step == 0:
            near[...] = spread
            own_squares[...] = spread
        else:
            others[2 * step - 2][:, :width] = total[rows]
            others[2 * step - 2][:, width:] = spread
            others[2 * step - 1][...] = spread


def totals(parts, ex_count):
    count, width = parts[0].shape
    per_ex = count // ex_count
    shape = lambda columns: jax.ShapeDtypeStruct((per_ex, columns), jnp.float32)
    near, *others, own_rows, own_squares = pl.pallas_call(
        functools.partial(total_body, ex_count),
        out_shape=[shape(128)] + [shape(width + 128), shape(128)] * (ex_count - 1) + [shape(width), shape(128)],
        in_specs=[VMEM] * len(parts),
        out_specs=[VMEM] * (2 * ex_count + 1),
        compiler_params=params(8),
    )(*parts)
    return [own_rows, *others[::2]], [near, *others[1::2]], own_squares


def scale_body(near_count, ex_count, columns, *refs):
    rows, squares, out = refs[near_count : near_count + ex_count], refs[:near_count] + refs[near_count + ex_count : -1], refs[-1]
    width = rows[0].shape[1]
    total = squares[0][...]
    for square in squares[1:]:
        total = total + square[...]
    for row in rows[1:]:
        total = total + row[:, width:]
    norm = jnp.sqrt(total[:, :1] / columns + 1e-06)
    for step in range(ex_count):
        place = place_at(lax.axis_index("ex"), ex_count, step, -1)
        out[:, pl.ds(pl.multiple_of(place * width, 128), width)] = rows[step][:, :width] / norm


def scale(near, rows, squares, columns):
    per_ex, width = rows[0].shape
    operands = (*near, *rows, *squares)
    return pl.pallas_call(
        functools.partial(scale_body, len(near), len(rows), columns),
        out_shape=jax.ShapeDtypeStruct((per_ex, width * len(rows)), jnp.float32),
        in_specs=[VMEM] * len(operands),
        out_specs=VMEM,
        compiler_params=params(8),
    )(*operands)


def per_device(hidden, cotangent, adapter_down_factor, projection, lengths, slot_example_order):
    counts = ctx_count, feat_count, ex_count = tuple(map(lax.axis_size, ("ctx", "feat", "ex")))
    ctx_steps = sorted(range(1, ctx_count), key=lambda s: (s == 1, s))
    chip_steps = exchange_steps(feat_count, ex_count)[1:]

    *blocks, ranks, share = gradient(
        hidden, adapter_down_factor.T, cotangent, projection, lengths, slot_example_order, counts
    )
    shares = [share, load(projection, 1, ex_count, ranks)]
    grad_rows = sum_rows(
        [blocks[0]] + [swap(blocks[s], ("ctx",), (s,)) for s in ctx_steps], jnp.bfloat16, shares[1]
    )
    shares.append(load(projection, 2, ex_count, grad_rows))
    sources = [grad_rows] + [swap(grad_rows, ("feat", "ex"), s) for s in chip_steps]
    product = project(sources, ranks, projection, shares, ex_count)
    rows, squares, own_squares = totals([product] + [swap(product, ("ctx",), (s,)) for s in reversed(ctx_steps)], ex_count)
    taken = [rows[0]] + [swap(rows[s], ("ex",), (s,)) for s in range(1, ex_count)]
    near, far = (
        [swap(squares[e], ("feat", "ex"), (f, e)) for f, e in chip_steps if f and bool(e) == both] for both in (False, True)
    )
    return scale(near, taken, [*far, own_squares], projection.shape[1] * feat_count)


def solution(mesh):
    in_specs = (
        P(("group", "feat", "ex"), "ctx", None),
        P(("group", "feat", "ex"), "ctx", None),
        P(),
        P("ctx", "feat"),
        P(("group", "feat", "ex")),
        P("group"),
    )
    out_specs = P(("group", "ex"), "feat")
    return jax.shard_map(
        per_device, mesh=mesh, in_specs=in_specs, out_specs=out_specs, check_vma=False
    )
```

```python
import functools
import itertools

import jax
import jax.numpy as jnp
from jax import lax
from jax.experimental import pallas as pl
from jax.experimental.pallas import tpu as pltpu
from jax.sharding import PartitionSpec as P

MIB = 1 << 20
SHARES = (3, 2, 3)
VMEM = pl.BlockSpec(memory_space=pltpu.VMEM)
HBM = pl.BlockSpec(memory_space=pltpu.HBM)


def is_power(count):
    return count & (count - 1) == 0


def place_at(index, count, step, sign=1):
    if is_power(count):
        return index ^ step
    return (index + sign * step + count) % count


def step_to(index, target, count):
    if is_power(count):
        return index ^ target
    return lax.rem(target - index + count, count)


def exchange_steps(feat_count, ex_count):
    steps = itertools.product(range(feat_count), range(ex_count))
    return sorted(steps, key=lambda s: (any(s), not all(s), s))


def swap(value, axes, steps):
    sizes = [lax.axis_size(a) for a in axes]
    flat = lambda place: functools.reduce(lambda total, p: total * p[1] + p[0], zip(place, sizes), 0)
    pairs = [
        (flat(place), flat([place_at(i, n, s) for i, n, s in zip(place, sizes, steps)]))
        for place in itertools.product(*map(range, sizes))
    ]
    return lax.ppermute(value, tuple(axes) if len(axes) > 1 else axes[0], pairs)


def params(mib, **more):
    return pltpu.CompilerParams(vmem_limit_bytes=mib * MIB, **more)


def lane_dot(a, b):
    return lax.dot_general(a, b, (((1,), (1,)), ((), ())), preferred_element_type=jnp.float32)


def hbm(value):
    return pltpu.with_memory_space_constraint(value, pltpu.HBM)


def share_rows(depth, number):
    eighth = depth // sum(SHARES)
    return sum(SHARES[:number]) * eighth, SHARES[number] * eighth


def share_copy(projection_hbm, buffer, sem, number):
    first, rows = share_rows(projection_hbm.shape[0], number)
    width = buffer.shape[1]
    columns = pl.ds(pl.multiple_of(lax.axis_index("ex") * width, 128), width)
    return pltpu.make_async_copy(projection_hbm.at[pl.ds(first, rows), columns], buffer, sem)


def share_shape(projection, number, ex_count):
    depth, width = projection.shape
    return share_rows(depth, number)[1], width // ex_count


def load_body(number, after_ref, projection_hbm, buffer, sem):
    copy = share_copy(projection_hbm, buffer, sem, number)
    copy.start()
    copy.wait()


def load(projection, number, ex_count, after):
    return pl.pallas_call(
        functools.partial(load_body, number),
        out_shape=pltpu.VMEM(share_shape(projection, number, ex_count), projection.dtype),
        in_specs=[VMEM, HBM],
        out_specs=VMEM,
        scratch_shapes=[pltpu.SemaphoreType.DMA],
        compiler_params=params(2),
    )(after, hbm(projection))


def gradient_body(chunks, counts, hidden_hbm, factor_hbm, cotangent_hbm, projection_hbm, lengths, order_hbm, *refs):
    ctx_count, feat_count, ex_count = counts
    outs, ranks_ref, share_ref = refs[:ctx_count], refs[ctx_count], refs[ctx_count + 1]
    hidden, factor, cotangent, blocks, order, sems, order_sem = refs[ctx_count + 2 :]
    own, tokens, width = hidden.shape
    part = width // chunks
    order_copy = pltpu.make_async_copy(order_hbm, order, order_sem)
    order_copy.start()
    copies = [pltpu.make_async_copy(factor_hbm, factor, sems.at[0])]
    for k in range(chunks):
        columns = pl.ds(k * part, part)
        copies.append(
            pltpu.make_async_copy(hidden_hbm.at[:, :, columns], hidden.at[:, :, columns], sems.at[1 + k])
        )
    copies.append(pltpu.make_async_copy(cotangent_hbm, cotangent, sems.at[1 + chunks]))
    copies.append(share_copy(projection_hbm, share_ref, sems.at[2 + chunks], 0))
    for copy in copies:
        copy.start()
    copies[0].wait()
    down = [None] * own
    for k in range(chunks):
        copies[1 + k].wait()
        for e in range(own):
            product = lane_dot(factor[:, k * part : (k + 1) * part], hidden[e, :, k * part : (k + 1) * part])
            down[e] = product if k == 0 else down[e] + product
    copies[-2].wait()
    order_copy.wait()
    place = lax.axis_index("ctx")
    for e in range(own):
        rows = down[e].astype(jnp.bfloat16)
        position = place * tokens + lax.broadcasted_iota(jnp.int32, rows.shape, 1)
        rows = jnp.where(position < lengths[e], rows.astype(jnp.float32), 0.0).astype(jnp.bfloat16)
        grad = jnp.dot(rows, cotangent[e], preferred_element_type=jnp.float32)
        share = grad.shape[0] // ctx_count
        for c in range(ctx_count):
            blocks[c, e] = grad[c * share : (c + 1) * share]
    for step in range(ctx_count):
        outs[step][...] = blocks[place_at(place, ctx_count, step)]
    feat, ex = lax.axis_index("feat"), lax.axis_index("ex")
    per_ex = own * feat_count
    for k, steps in enumerate(exchange_steps(feat_count, ex_count)):
        from_feat, from_ex = place_at(feat, feat_count, steps[0], -1), place_at(ex, ex_count, steps[1], -1)
        for e in range(own):
            wanted = order[(from_feat * ex_count + from_ex) * own + e]
            rank = step_to(ex, lax.div(wanted, per_ex), ex_count) * per_ex + lax.rem(wanted, per_ex)
            ranks_ref[pl.ds(k * own + e, 1), :] = jnp.full((1, 128), rank, jnp.int32)
    copies[-1].wait()


def gradient(hidden, factor, cotangent, projection, lengths, order, counts):
    ctx_count, feat_count, ex_count = counts
    own, tokens, width = hidden.shape
    rank, model = factor.shape[0], cotangent.shape[2]
    shape = (own, rank // ctx_count, model)
    chunks = 2
    return pl.pallas_call(
        functools.partial(gradient_body, chunks, counts),
        out_shape=[jax.ShapeDtypeStruct(shape, jnp.float32)] * ctx_count
        + [
            jax.ShapeDtypeStruct((own * feat_count * ex_count, 128), jnp.int32),
            pltpu.VMEM(share_shape(projection, 0, ex_count), projection.dtype),
        ],
        in_specs=[HBM] * 4 + [pl.BlockSpec(memory_space=pltpu.SMEM), HBM],
        out_specs=[VMEM] * (ctx_count + 2),
        scratch_shapes=[
            pltpu.VMEM(hidden.shape, hidden.dtype),
            pltpu.VMEM(factor.shape, factor.dtype),
            pltpu.VMEM(cotangent.shape, cotangent.dtype),
            pltpu.VMEM((ctx_count,) + shape, jnp.float32),
            pltpu.SMEM(order.shape, order.dtype),
            pltpu.SemaphoreType.DMA((chunks + 3,)),
            pltpu.SemaphoreType.DMA,
        ],
        compiler_params=params(8),
    )(*map(hbm, (hidden, factor, cotangent, projection)), lengths, hbm(order))


def sum_body(*refs):
    total = refs[0][...]
    for ref in refs[1:-2]:
        total = total + ref[...]
    refs[-1][...] = total.astype(refs[-1].dtype)


def sum_rows(parts, dtype, after):
    return pl.pallas_call(
        sum_body,
        out_shape=jax.ShapeDtypeStruct(parts[0].shape, dtype),
        in_specs=[VMEM] * (len(parts) + 1),
        out_specs=VMEM,
        compiler_params=params(2),
    )(*parts, pltpu.with_memory_space_constraint(after, pltpu.VMEM))


def project_body(source_count, ranks_ref, *refs):
    sources, shares, (out, rows_ref) = refs[:source_count], refs[source_count:-2], refs[-2:]
    padded, count = rows_ref.shape[0], out.shape[0]
    own, share, model = sources[0].shape
    row = lax.broadcasted_iota(jnp.int32, (padded, model), 0)
    ranks = ranks_ref[...][:, :1]
    for r in range(share):
        rows = jnp.zeros((padded, model), jnp.float32)
        for k, source in enumerate(sources):
            for e in range(own):
                values = source[e, r : r + 1].astype(jnp.float32)
                rows = rows + jnp.where(row == ranks[k * own + e : k * own + e + 1], values, 0.0)
        rows_ref[:, r * model : (r + 1) * model] = rows.astype(jnp.bfloat16)
    for number, weights in enumerate(shares):
        first, depth = share_rows(rows_ref.shape[1], number)
        part = jnp.dot(rows_ref[:, first : first + depth], weights[...], preferred_element_type=jnp.float32)
        total = part if number == 0 else total + part
    out[...] = total[:count]


def project(sources, ranks, projection, shares, ex_count):
    depth, width = projection.shape
    count = ranks.shape[0]
    padded = max(8, count)
    return pl.pallas_call(
        functools.partial(project_body, len(sources)),
        out_shape=jax.ShapeDtypeStruct((count, width // ex_count), jnp.float32),
        in_specs=[VMEM] * (1 + len(sources) + len(shares)),
        out_specs=VMEM,
        scratch_shapes=[
            pltpu.VMEM((padded, depth), jnp.bfloat16),
        ],
        compiler_params=params(8),
    )(ranks, *sources, *[pltpu.with_memory_space_constraint(v, pltpu.VMEM) for v in shares])


def total_body(ex_count, *refs):
    parts = refs[: -2 * ex_count - 1]
    near, *others, own_rows, own_squares = refs[-2 * ex_count - 1 :]
    total = parts[0][...]
    for part in parts[1:]:
        total = total + part[...]
    squares = jnp.sum(total * total, axis=1, keepdims=True)
    per_ex, width = own_rows.shape
    own_rows[...] = total[:per_ex]
    for step in range(ex_count):
        rows = slice(step * per_ex, (step + 1) * per_ex)
        spread = jnp.broadcast_to(squares[rows], (per_ex, 128))
        if step == 0:
            near[...] = spread
            own_squares[...] = spread
        else:
            others[2 * step - 2][:, :width] = total[rows]
            others[2 * step - 2][:, width:] = spread
            others[2 * step - 1][...] = spread


def totals(parts, ex_count):
    count, width = parts[0].shape
    per_ex = count // ex_count
    shape = lambda columns: jax.ShapeDtypeStruct((per_ex, columns), jnp.float32)
    near, *others, own_rows, own_squares = pl.pallas_call(
        functools.partial(total_body, ex_count),
        out_shape=[shape(128)] + [shape(width + 128), shape(128)] * (ex_count - 1) + [shape(width), shape(128)],
        in_specs=[VMEM] * len(parts),
        out_specs=[VMEM] * (2 * ex_count + 1),
        compiler_params=params(8),
    )(*parts)
    return [own_rows, *others[::2]], [near, *others[1::2]], own_squares


def scale_body(near_count, ex_count, columns, *refs):
    rows, squares, out = refs[near_count : near_count + ex_count], refs[:near_count] + refs[near_count + ex_count : -1], refs[-1]
    width = rows[0].shape[1]
    total = squares[0][...]
    for square in squares[1:]:
        total = total + square[...]
    for row in rows[1:]:
        total = total + row[:, width:]
    norm = jnp.sqrt(total[:, :1] / columns + 1e-06)
    for step in range(ex_count):
        place = place_at(lax.axis_index("ex"), ex_count, step, -1)
        out[:, pl.ds(pl.multiple_of(place * width, 128), width)] = rows[step][:, :width] / norm


def scale(near, rows, squares, columns):
    per_ex, width = rows[0].shape
    operands = (*near, *rows, *squares)
    return pl.pallas_call(
        functools.partial(scale_body, len(near), len(rows), columns),
        out_shape=jax.ShapeDtypeStruct((per_ex, width * len(rows)), jnp.float32),
        in_specs=[VMEM] * len(operands),
        out_specs=VMEM,
        compiler_params=params(8),
    )(*operands)


def per_device(hidden, cotangent, adapter_down_factor, projection, lengths, slot_example_order):
    counts = ctx_count, feat_count, ex_count = tuple(map(lax.axis_size, ("ctx", "feat", "ex")))
    ctx_steps = sorted(range(1, ctx_count), key=lambda s: (s == 1, s))
    chip_steps = exchange_steps(feat_count, ex_count)[1:]

    *blocks, ranks, share = gradient(
        hidden, adapter_down_factor.T, cotangent, projection, lengths, slot_example_order, counts
    )
    shares = [share, load(projection, 1, ex_count, ranks)]
    grad_rows = sum_rows(
        [blocks[0]] + [swap(blocks[s], ("ctx",), (s,)) for s in ctx_steps], jnp.bfloat16, shares[1]
    )
    shares.append(load(projection, 2, ex_count, grad_rows))
    sources = [grad_rows] + [swap(grad_rows, ("feat", "ex"), s) for s in chip_steps]
    product = project(sources, ranks, projection, shares, ex_count)
    rows, squares, own_squares = totals([product] + [swap(product, ("ctx",), (s,)) for s in reversed(ctx_steps)], ex_count)
    taken = [rows[0]] + [swap(rows[s], ("ex",), (s,)) for s in range(1, ex_count)]
    near, far = (
        [swap(squares[e], ("feat", "ex"), (f, e)) for f, e in chip_steps if f and bool(e) == both] for both in (False, True)
    )
    return scale(near, taken, [*far, own_squares], projection.shape[1] * feat_count)


def solution(mesh):
    in_specs = (
        P(("group", "feat", "ex"), "ctx", None),
        P(("group", "feat", "ex"), "ctx", None),
        P(),
        P("ctx", "feat"),
        P(("group", "feat", "ex")),
        P("group"),
    )
    out_specs = P(("group", "ex"), "feat")
    return jax.shard_map(
        per_device, mesh=mesh, in_specs=in_specs, out_specs=out_specs, check_vma=False
    )
```
